32 devices in a mesh: groups: 2 (over y), row: 4 (over z), col: 2 (over x), mode: 2 (over core).
Axes of the slice: x: 2, y: 2, z: 4, core: 2. Of those that a mesh axis runs over, the one named last changes fastest.
Arguments:
- object_field: float32 [2048, 2, 1024], P(('groups', 'row'), None, 'col'), parts along dimension 0, may hold values from -12 to 12
- probe_field: float32 [512, 2, 256], P('groups'), parts along dimension 0, may hold values from -5 to 5
- amplitudes: bfloat16 [128, 256, 256], P(('groups', 'row', 'col', 'mode')), parts along dimension 0
- row_offset: int32 [128], P(('groups', 'row', 'col', 'mode')), parts along dimension 0, may hold values from 0 to 768, as said below
- col_offset: int32 [128], P(('groups', 'row', 'col', 'mode')), parts along dimension 0, may hold values from 0 to 768, as said below
- counts: int32 [32], P(('groups', 'row', 'col', 'mode')), parts along dimension 0, may hold values from 1 to 4
Outputs:
- object_new: float32 [2048, 2, 1024], P(('groups', 'row', 'mode'), None, 'col'), parts along dimension 0
- probe_new: float32 [512, 2, 256], P('groups'), parts along dimension 0
The draws below stay inside these ranges and needn't reach their ends.
There are 2 independent parts, one for each index of `groups`. The reference program is written for one: setup_inputs(seed, part) draws one part's arguments, and reference() takes and returns one part's arrays. A program takes and returns all parts, laid end to end along the dimension named above; each array names one. Nothing has to cross between parts.
Inputs may be any that keep to these rules, and one draw needn't show every extreme that they name: `row_offset`: slot j lies on device j div 4 of row+col+mode; its patch starts inside that device's object tile of 256 rows, on a multiple of 64, and stays inside the object. `col_offset`: its patch starts inside the device's tile of 512 columns, on a multiple of 64, and stays inside the object.
All inputs are finite; a program needn't handle non-finite values.
Results may differ from the reference program's by a relative error of at most 0.0007.
The reference program's roundings to bfloat16 on the way count: a program that leaves them out, or rounds other values in their place, can miss the bound.
Values may be sent and summed in bfloat16 or wider, within the bound.
A program may use at most 64 MiB of HBM per device.

```python
import math
import jax
import jax.numpy as jnp
from jax import lax

FRAME = 256
TILE_R = 256
TILE_C = 512
POS_DEV = 4
OBJ_R = 1024
OBJ_C = 1024
DEV_PART = 16
POSITIONS = 64


def offsets_within(key, device_ids, slot_within, tile_ids, tiles_count, extent):
    raster_step = FRAME // 4
    limit = jnp.where(tile_ids == tiles_count - 1, extent - FRAME + 1, extent).astype(jnp.int32)
    points = ((limit - 1) // raster_step + 1).astype(jnp.int32)
    raw_index = jax.random.randint(jax.random.fold_in(key, 1), device_ids.shape, 0, points).astype(jnp.int32)
    favored = jax.random.randint(jax.random.fold_in(key, 3), (), 0, 4).astype(jnp.int32)
    take_favored = jax.random.randint(jax.random.fold_in(key, 4), device_ids.shape, 0, 2) == 1
    aligned = favored + 4 * (raw_index // 4)
    index = jnp.where(take_favored & (aligned < points), aligned, raw_index)
    picks = jax.random.randint(jax.random.fold_in(key, 2), (DEV_PART,), 0, POS_DEV).astype(jnp.int32)
    chosen = picks[device_ids]
    index = jnp.where(slot_within == chosen, points - 1, index)
    index = jnp.where(slot_within == (chosen + 1) % POS_DEV, 0, index)
    return (tile_ids * extent + index * raster_step).astype(jnp.int32)


def draw_row_offset(key, part):
    slot_ids = jnp.arange(POSITIONS, dtype=jnp.int32)
    device_ids = slot_ids // POS_DEV
    rows_count = OBJ_R // TILE_R
    per_row = DEV_PART // rows_count
    tile_ids = device_ids // per_row
    return offsets_within(jax.random.fold_in(key, 11), device_ids, slot_ids % POS_DEV, tile_ids, rows_count, TILE_R)


def draw_col_offset(key, part):
    slot_ids = jnp.arange(POSITIONS, dtype=jnp.int32)
    device_ids = slot_ids // POS_DEV
    rows_count = OBJ_R // TILE_R
    cols_count = OBJ_C // TILE_C
    modes_count = DEV_PART // (rows_count * cols_count)
    tile_ids = device_ids // modes_count % cols_count
    return offsets_within(jax.random.fold_in(key, 12), device_ids, slot_ids % POS_DEV, tile_ids, cols_count, TILE_C)


def draw_counts(key, part):
    first_draw = jax.random.randint(jax.random.fold_in(key, 21), (DEV_PART,), 0, POS_DEV)
    second_draw = jax.random.randint(jax.random.fold_in(key, 22), (DEV_PART,), 0, POS_DEV)
    base_count = 1 + jnp.minimum(first_draw, second_draw)
    phase_pick = jax.random.randint(jax.random.fold_in(key, 23), (), 0, 8)
    device_ids = jnp.arange(DEV_PART, dtype=jnp.int32)
    return jnp.where(device_ids % 8 == phase_pick, POS_DEV, base_count).astype(jnp.int32)


def draw_amplitudes(key, part):
    position_frac = jnp.arange(POSITIONS, dtype=jnp.float32) / max(POSITIONS - 1, 1)
    frame_gain = jax.random.uniform(jax.random.fold_in(key, 31), (POSITIONS, 1, 1), minval=0.7, maxval=1.4)
    ramp_values = 1.0 + 2.0 * position_frac
    normal_values = jnp.clip(jax.random.normal(jax.random.fold_in(key, 33), (POSITIONS, FRAME, FRAME)), -5.0, 5.0)
    values = jnp.abs(normal_values) * 1.25
    return (values * frame_gain * ramp_values[:, None, None]).astype(jnp.bfloat16)


def draw_object_field(key, part):
    normal_values = jnp.clip(jax.random.normal(jax.random.fold_in(key, 41), (OBJ_R, 2, OBJ_C)), -5.0, 5.0) * 0.7
    return normal_values.astype(jnp.float32)


def noise(own_key, shape, deviation, bound, kind=jnp.bfloat16):
    entries = jax.random.normal(own_key, shape, jnp.float32) * deviation
    return jnp.minimum(jnp.maximum(entries, -bound), bound).astype(kind)


def setup_inputs(seed: int = 0, part: int = 0) -> dict:
    arg_keys = jax.random.split(jax.random.key(seed), 7)
    part_keys = jax.random.split(jax.random.fold_in(arg_keys[6], part), 7)
    return {
        "object_field": draw_object_field(jax.random.fold_in(jax.random.fold_in(arg_keys[6], part), 71), part),
        "probe_field": noise(part_keys[1], (FRAME, 2, FRAME), 0.7, 5.0, jnp.float32),
        "amplitudes": draw_amplitudes(jax.random.fold_in(jax.random.fold_in(arg_keys[6], part), 71), part),
        "row_offset": draw_row_offset(jax.random.fold_in(jax.random.fold_in(arg_keys[6], part), 71), part),
        "col_offset": draw_col_offset(jax.random.fold_in(jax.random.fold_in(arg_keys[6], part), 71), part),
        "counts": draw_counts(jax.random.fold_in(jax.random.fold_in(arg_keys[6], part), 71), part),
    }


MODULUS_FLOOR = 0.5
EPSILON = 1e-05
REGULARIZER = 1.0

def dft_table(points, sign):
    freq_index = jnp.arange(points, dtype=jnp.int32)
    product = freq_index[:, None] * freq_index[None, :] % points
    angle_grid = 2.0 * math.pi / points * product.astype(jnp.float32)
    norm_factor = 1.0 / math.sqrt(points)
    cosine = jnp.cos(angle_grid) * norm_factor
    sine_part = jnp.sin(angle_grid) * (sign * norm_factor)
    upper_rows = jnp.stack([cosine, sine_part], axis=-1)
    lower_rows = jnp.stack([-sine_part, cosine], axis=-1)
    return jnp.stack([upper_rows, lower_rows], axis=1).astype(jnp.bfloat16)

def transform(frames, dft_matrix):
    wide_table = dft_matrix.astype(jnp.float32)
    frames = lax.optimization_barrier(frames)
    first_pass = jnp.einsum('kanb,nbm->kam', wide_table, frames.astype(jnp.float32), precision=lax.Precision.HIGHEST)
    first_pass = lax.optimization_barrier(first_pass.astype(jnp.bfloat16)).astype(jnp.float32)
    return jnp.einsum('kbm,lamb->kal', first_pass, wide_table, precision=lax.Precision.HIGHEST)

def frame_update(obj_patch, probe_field, amplitude, forward, inverse):
    obj_re = obj_patch[:, 0, :].astype(jnp.float32)
    obj_im = obj_patch[:, 1, :].astype(jnp.float32)
    probe_re = probe_field[:, 0, :]
    probe_im = probe_field[:, 1, :]
    exit_wave = jnp.stack([probe_re * obj_re - probe_im * obj_im, probe_re * obj_im + probe_im * obj_re], axis=1).astype(jnp.bfloat16)
    far_field = transform(exit_wave, forward)
    modulus = jnp.sqrt(far_field[:, 0, :] ** 2 + far_field[:, 1, :] ** 2)
    factor = amplitude.astype(jnp.float32) / jnp.maximum(modulus, MODULUS_FLOOR) - 1.0
    change = (far_field * factor[:, None, :]).astype(jnp.bfloat16)
    back_field = transform(change, inverse)
    chi_re = back_field[:, 0, :]
    chi_im = back_field[:, 1, :]
    obj_step = jnp.stack([probe_re * chi_re + probe_im * chi_im, probe_re * chi_im - probe_im * chi_re], axis=1)
    grad_re = obj_re * chi_re + obj_im * chi_im
    grad_im = obj_re * chi_im - obj_im * chi_re
    weight = obj_re * obj_re + obj_im * obj_im
    return (obj_step, grad_re, grad_im, weight)

def reference(object_field, probe_field, amplitudes, row_offset, col_offset, counts):
    forward = dft_table(FRAME, 1.0)
    inverse = dft_table(FRAME, -1.0)
    object_half = lax.optimization_barrier(object_field.astype(jnp.bfloat16))
    slot_ids = jnp.arange(POSITIONS, dtype=jnp.int32)
    live_mask = (slot_ids % POS_DEV < counts[slot_ids // POS_DEV]).astype(jnp.float32)

    def scan_step(state_now, scan_item):
        update_sum, grad_re, grad_im, weight_sum = state_now
        amplitude, top_row, left_col, live_flag = scan_item
        start = (top_row.astype(jnp.int32), jnp.int32(0), left_col.astype(jnp.int32))
        obj_patch = lax.dynamic_slice(object_half, start, (FRAME, 2, FRAME))
        obj_step, part_re, part_im, weight = frame_update(obj_patch, probe_field, amplitude, forward, inverse)
        current = lax.dynamic_slice(update_sum, start, (FRAME, 2, FRAME))
        update_sum = lax.dynamic_update_slice(update_sum, current + live_flag * obj_step, start)
        return ((update_sum, grad_re + live_flag * part_re, grad_im + live_flag * part_im, weight_sum + live_flag * weight), None)
    zero_frame = jnp.zeros((FRAME, FRAME), jnp.float32)
    initial = (jnp.zeros(object_field.shape, jnp.float32), zero_frame, zero_frame, zero_frame)
    final_state, _ = lax.scan(scan_step, initial, (amplitudes, row_offset, col_offset, live_mask))
    update_sum, grad_re, grad_im, weight_sum = final_state
    probe_peak = jnp.max(probe_field[:, 0, :] ** 2 + probe_field[:, 1, :] ** 2) + EPSILON
    object_new = object_field + update_sum / probe_peak
    denominator = weight_sum + REGULARIZER
    probe_new = probe_field + jnp.stack([grad_re / denominator, grad_im / denominator], axis=1)
    return (object_new, probe_new)
```

```python
import functools
import math

import jax
import jax.numpy as jnp
import numpy as np
from jax import lax
from jax.experimental import pallas as pl
from jax.experimental.pallas import tpu as pltpu
from jax.sharding import PartitionSpec as P

FLOOR_SQUARED = 0.25
EPSILON = 1e-05
REGULARIZER = 1.0
F32 = jnp.float32
BF16 = jnp.bfloat16
MESH = pl.DeviceIdType.MESH
VMEM = pltpu.VMEM
LANES = 128
SHIFT = 64
CODE_BITS = 14
CODE_BIAS = 120
GROUP = 4


def dft_tables(points):
    index = np.arange(points)
    product = (index[:, None] * index[None, :]) % points
    angle = (2.0 * math.pi / points) * product.astype(np.float32)
    norm = np.float32(1.0 / math.sqrt(points))
    cosine = (np.cos(angle.astype(np.float32)) * norm).astype(np.float32)
    sine = (np.sin(angle.astype(np.float32)) * norm).astype(np.float32)
    first = np.block([[cosine, sine], [-sine, cosine]])
    second = np.block([[cosine, -sine], [sine, cosine]])
    return jnp.asarray(first, BF16), jnp.asarray(second, BF16)


def greet(peers):
    barrier = pltpu.get_barrier_semaphore()
    expected = jnp.int32(0)
    for present, where in peers:
        expected = expected + present.astype(jnp.int32)

        @pl.when(present)
        def _(where=where):
            pl.semaphore_signal(barrier, inc=1, device_id=where, device_id_type=MESH)

    return expected


def remote(src, dst, sems, slot, where):
    return pltpu.make_async_remote_copy(
        src_ref=src,
        dst_ref=dst,
        send_sem=sems.at[0, slot],
        recv_sem=sems.at[1, slot],
        device_id=where,
        device_id_type=MESH,
    )


def halo_kernel(rows_n, cols_n, count, *refs):
    field_hbm, probe_hbm = refs[:2]
    extras = refs[2 : 2 + count]
    obj_ref, planes_ref, acc_ref = refs[2 + count : 5 + count]
    landed = refs[5 + count : 5 + 2 * count]
    field_ref, probe_ref, sems, local = refs[5 + 2 * count :]
    r = lax.axis_index("row")
    c = lax.axis_index("col")
    m = lax.axis_index("mode")
    tile_r, _, tile_c = field_ref.shape
    frame = probe_ref.shape[0]
    half, reach = tile_r // 2, frame - SHIFT
    low = reach // 2
    soon = tile_r - low
    early = pl.ds(pl.multiple_of(m * low, 32), soon)
    late = pl.ds(pl.multiple_of((1 - m) * soon, 32), low)
    pairs = [(field_hbm.at[early], field_ref.at[early]), (field_hbm.at[late], field_ref.at[late])]
    pairs += [(probe_hbm, probe_ref), *zip(extras, landed)]
    fetches = [pltpu.make_async_copy(a, b, local.at[i]) for i, (a, b) in enumerate(pairs)]
    for fetch in fetches:
        fetch.start()
    has_up, has_down = r > 0, r < rows_n - 1
    has_left, has_right = c > 0, c < cols_n - 1
    sib = {"mode": 1 - m}
    up, down = {"row": r - 1}, {"row": r + 1}
    left, right = {"col": c - 1}, {"col": c + 1}
    always = m >= 0
    peers = [(always, sib), (has_up, up), (has_down, down), (has_left, left), (has_right, right)]
    expected = greet(peers)
    mine = pl.ds(pl.multiple_of(m * half, half), half)
    lift = pl.ds(pl.multiple_of(m * low, 32), low)
    below = pl.ds(pl.multiple_of(tile_r + m * low, 32), low)
    first, rest, edge = pl.ds(0, frame), pl.ds(frame, tile_c - frame), pl.ds(tile_c, frame)

    def part(rows, cols, to_rows, to_cols, slot, where):
        return remote(
            obj_ref.at[:, rows, cols], obj_ref.at[:, to_rows, to_cols], sems, slot, where
        )

    up_first = part(lift, first, below, first, 0, up)
    to_left = part(mine, first, mine, edge, 1, left)
    up_rest = part(lift, rest, below, rest, 2, up)
    corner = part(below, first, below, edge, 3, left)
    swap_edge = part(mine, edge, mine, edge, 4, sib)
    swap_first = part(below, first, below, first, 5, sib)
    swap_rest = part(below, rest, below, rest, 6, sib)
    swap_corner = part(below, edge, below, edge, 7, sib)

    def convert(rows):
        for plane in range(2):
            obj_ref[plane, rows, :tile_c] = field_ref[rows, plane, :].astype(BF16)

    fetches[0].wait()
    convert(early)
    pl.semaphore_wait(pltpu.get_barrier_semaphore(), expected)

    @pl.when(has_up)
    def _():
        up_first.start()

    @pl.when(has_left)
    def _():
        to_left.start()

    @pl.when(has_up)
    def _():
        up_rest.start()

    fetches[1].wait()
    convert(late)
    fetches[2].wait()
    for plane in range(2):
        planes_ref[plane] = probe_ref[:, plane, :]
    acc_ref[...] = jnp.zeros(acc_ref.shape, F32)

    @pl.when(has_down)
    def _():
        up_first.wait_recv()

        @pl.when(has_left)
        def _():
            corner.start()

        swap_first.start()

    @pl.when(has_right)
    def _():
        to_left.wait_recv()
        swap_edge.start()

    @pl.when(has_down)
    def _():
        up_rest.wait_recv()
        swap_rest.start()

    @pl.when(has_right & has_down)
    def _():
        corner.wait_recv()
        swap_corner.start()
        swap_corner.wait()

    @pl.when(has_right)
    def _():
        swap_edge.wait()

    @pl.when(has_down)
    def _():
        swap_first.wait()
        swap_rest.wait()

        @pl.when(has_left)
        def _():
            corner.wait_send()

    @pl.when(has_left)
    def _():
        to_left.wait_send()

    @pl.when(has_up)
    def _():
        up_first.wait_send()
        up_rest.wait_send()

    for fetch in fetches[3:]:
        fetch.wait()


def halo(field, probe, extras, rows_n, cols_n):
    tile_r, planes, tile_c = field.shape
    frame = probe.shape[0]
    shape = (planes, tile_r + frame, tile_c + frame)
    in_vmem = pl.BlockSpec(memory_space=VMEM)
    return pl.pallas_call(
        functools.partial(halo_kernel, rows_n, cols_n, len(extras)),
        out_shape=(
            jax.ShapeDtypeStruct(shape, BF16),
            jax.ShapeDtypeStruct((planes, frame, frame), F32),
            jax.ShapeDtypeStruct(shape, F32),
            *(jax.ShapeDtypeStruct(x.shape, x.dtype) for x in extras),
        ),
        in_specs=[pl.BlockSpec(memory_space=pltpu.HBM)] * (2 + len(extras)),
        out_specs=(in_vmem,) * (3 + len(extras)),
        scratch_shapes=[
            VMEM(field.shape, F32),
            VMEM(probe.shape, F32),
            pltpu.SemaphoreType.DMA((2, 8)),
            pltpu.SemaphoreType.DMA((3 + len(extras),)),
        ],
        cost_estimate=pl.CostEstimate(flops=0, bytes_accessed=40 << 20, transcendentals=0),
        compiler_params=pltpu.CompilerParams(
            collective_id=0, has_side_effects=True, vmem_limit_bytes=8 << 20
        ),
        name="halo",
    )(*(pltpu.with_memory_space_constraint(x, pltpu.HBM) for x in (field, probe, *extras)))


def frames_kernel(
    row_ref, col_ref, count_ref, obj, probe_ref, amp_ref, first_ref, second_ref, _zero,
    acc, sum_ref, patch, tall, wide, field,
):
    frame = probe_ref.shape[1]
    ext_rows, ext_cols = obj.shape[1:]
    top = lax.axis_index("row") * (ext_rows - frame)
    left = lax.axis_index("col") * (ext_cols - frame)
    step = 32
    chunks = range(0, frame, step)
    tiles = frame // LANES
    lane = lax.broadcasted_iota(jnp.int32, (step, LANES), 1)
    sum_ref[...] = jnp.zeros_like(sum_ref)

    def place(slot):
        row = row_ref[slot] - top
        col = col_ref[slot] - left
        return row, (col // LANES) * LANES, col % LANES

    def columns(base, tile):
        return pl.ds(pl.multiple_of(base + tile * LANES, LANES), LANES)

    def enter(slot, at):
        row, base, shift = place(slot)
        for k in chunks:
            rows = pl.ds(pl.multiple_of(row + k, step), step)
            here = pl.ds(k, step)
            for plane in range(2):
                turned = []
                for tile in range(tiles + 1):
                    value = obj[plane, rows, columns(base, tile)].astype(F32)
                    turned.append(pltpu.roll(value, shift, 1))
                for tile in range(tiles):
                    value = jnp.where(lane < LANES - shift, turned[tile], turned[tile + 1])
                    patch[at, plane, here, tile * LANES : (tile + 1) * LANES] = value.astype(BF16)
            o_re, o_im = patch[at, 0, here, :].astype(F32), patch[at, 1, here, :].astype(F32)
            p_re, p_im = probe_ref[0, here, :], probe_ref[1, here, :]
            tall[at, here, :] = (p_re * o_re - p_im * o_im).astype(BF16)
            tall[at, frame + k : frame + k + step, :] = (p_re * o_im + p_im * o_re).astype(BF16)

    def transform(at, one_ref, two_ref):
        half = jnp.dot(one_ref[...], tall[at], preferred_element_type=F32).astype(BF16)
        wide[at, :, :frame] = half[:frame]
        wide[at, :, frame:] = half[frame:]
        field[at] = jnp.dot(wide[at], two_ref[...], preferred_element_type=F32)

    def constrain(slot, at):
        for k in chunks:
            here = pl.ds(k, step)
            f_re = field[at, here, :frame]
            f_im = field[at, here, frame:]
            amp = amp_ref[slot, here, :].astype(F32)
            power = f_re * f_re + f_im * f_im
            factor = amp * lax.rsqrt(jnp.maximum(power, FLOOR_SQUARED)) - 1.0
            tall[at, here, :] = (f_re * factor).astype(BF16)
            tall[at, frame + k : frame + k + step, :] = (f_im * factor).astype(BF16)

    def leave(slot, at):
        row, base, shift = place(slot)
        for k in chunks:
            rows = pl.ds(pl.multiple_of(row + k, step), step)
            here = pl.ds(k, step)
            x_re = field[at, here, :frame]
            x_im = field[at, here, frame:]
            p_re, p_im = probe_ref[0, here, :], probe_ref[1, here, :]
            o_re, o_im = patch[at, 0, here, :].astype(F32), patch[at, 1, here, :].astype(F32)
            for plane, value in enumerate((p_re * x_re + p_im * x_im, p_re * x_im - p_im * x_re)):
                turned = [
                    pltpu.roll(value[:, t * LANES : (t + 1) * LANES], shift, 1) for t in range(tiles)
                ]
                for tile in range(tiles + 1):
                    if tile == 0:
                        part = jnp.where(lane >= shift, turned[0], 0.0)
                    elif tile == tiles:
                        part = jnp.where(lane < shift, turned[-1], 0.0)
                    else:
                        part = jnp.where(lane < shift, turned[tile - 1], turned[tile])
                    acc[plane, rows, columns(base, tile)] += part
            sum_ref[0, here, :] += o_re * x_re + o_im * x_im
            sum_ref[1, here, :] += o_re * x_im - o_im * x_re
            sum_ref[2, here, :] += o_re * o_re + o_im * o_im

    def run(slots):
        for at, slot in enumerate(slots):
            enter(slot, at)
            transform(at, first_ref, second_ref)
        for at, slot in enumerate(slots):
            constrain(slot, at)
            transform(at, second_ref, first_ref)
        for at, slot in enumerate(slots):
            leave(slot, at)

    def pair(index, carry):
        run([index * GROUP + k for k in range(GROUP)])
        return carry

    count = count_ref[0]
    lax.fori_loop(0, count // GROUP, pair, 0)
    if GROUP > 1:
        lax.fori_loop((count // GROUP) * GROUP, count, lambda s, carry: (run([s]), carry)[1], 0)


def frames(row_offset, col_offset, counts, obj, probe, amplitudes, first, second, acc):
    frame = probe.shape[1]
    in_vmem = pl.BlockSpec(memory_space=VMEM)
    in_smem = pl.BlockSpec(memory_space=pltpu.SMEM)
    return pl.pallas_call(
        frames_kernel,
        out_shape=(
            jax.ShapeDtypeStruct(acc.shape, F32),
            jax.ShapeDtypeStruct((3, frame, frame), F32),
        ),
        in_specs=[in_smem] * 3 + [in_vmem] * 6,
        out_specs=(in_vmem, in_vmem),
        input_output_aliases={8: 0},
        scratch_shapes=[
            VMEM((GROUP, 2, frame, frame), BF16),
            VMEM((GROUP, 2 * frame, frame), BF16),
            VMEM((GROUP, frame, 2 * frame), BF16),
            VMEM((GROUP, frame, 2 * frame), F32),
        ],
        compiler_params=pltpu.CompilerParams(vmem_limit_bytes=14 << 20),
        name="frames",
    )(row_offset, col_offset, counts, obj, probe, amplitudes, first, second, acc)


def encode(value):
    rows = lax.broadcasted_iota(jnp.int32, value.shape, value.ndim - 2)
    peak = jnp.max(jnp.abs(value), axis=-2, keepdims=True)
    power = jnp.ceil(jnp.log2(jnp.maximum(peak, 1e-30)) + 0.01)
    bits = (power.astype(jnp.int32) + CODE_BIAS) >> (rows % 8)
    whole = jnp.round(value * jnp.exp2(CODE_BITS - power)).astype(jnp.int32)
    return (2 * whole + (bits & 1)).astype(jnp.int16)


def decode(code):
    code = code.astype(jnp.int32)
    rows = lax.broadcasted_iota(jnp.int32, code.shape, code.ndim - 2)
    low = code & 1
    bits = jnp.where(rows < 8, low << (rows % 8), 0)
    power = jnp.sum(bits, axis=-2, keepdims=True) - CODE_BIAS
    return (code - low).astype(F32) * jnp.exp2(power.astype(F32) - (CODE_BITS + 1))


def merge_kernel(
    rows_n, cols_n, with_probe, acc_ref, sum_ref, probe_ref, field_ref, share_ref, out_ref,
    got_corner, got_low, got_edge, got_top, total, low_left,
    right_corner, left_corner, right_edge, left_edge, to_down, from_up,
    got_sum, give, gotten, mine_code, sib_code, sems, psems, asems, fsems,
):
    r = lax.axis_index("row")
    c = lax.axis_index("col")
    m = lax.axis_index("mode")
    half, _, tile_c = share_ref.shape
    tile_r = 2 * half
    frame = probe_ref.shape[1]
    near = frame - SHIFT - half
    has_up, has_down = r > 0, r < rows_n - 1
    has_left, has_right = c > 0, c < cols_n - 1
    whole = m == 0
    sib = {"mode": 1 - m}
    up, down = {"row": r - 1}, {"row": r + 1}
    left, right = {"col": c - 1}, {"col": c + 1}
    always = m >= 0
    steps = [(a, b) for a in range(rows_n) for b in range(cols_n) if a or b]
    places = [(lax.rem(r + a, rows_n), lax.rem(c + b, cols_n)) for a, b in steps]
    peers = [{"row": a, "col": b} for a, b in places]
    if with_probe:
        expected = greet([(always, p) for p in [sib] + peers])
    else:
        near_by = [(has_up, up), (has_down, down), (has_left, left), (has_right, right)]
        expected = greet([(always, sib)] + near_by)
    pl.semaphore_wait(pltpu.get_barrier_semaphore(), expected)

    def block(which, base):
        return pl.ds(pl.multiple_of(which * half + base, half), half)

    top_mine, low_mine = block(m, 0), block(m, tile_r)
    top_sib, low_sib = block(1 - m, 0), block(1 - m, tile_r)
    body, edge = pl.ds(0, tile_c), pl.ds(tile_c, frame)
    first, rest = pl.ds(0, frame), pl.ds(frame, tile_c - frame)
    near_rows, far_rows = pl.ds(0, near), pl.ds(near, half - near)
    sum_rows = frame // 2
    shard = sum_rows // (rows_n * cols_n)

    def chip(row, col):
        return row * cols_n + col

    def rows_of(row, col, base=0):
        return pl.ds(pl.multiple_of(base + chip(row, col) * shard, shard), shard)

    if with_probe:
        away = pl.ds(pl.multiple_of((1 - m) * sum_rows, sum_rows), sum_rows)
        swap_sum = remote(sum_ref.at[:, away, :], got_sum, psems, 0, sib)
        swap_sum.start()
    swap_corner = remote(acc_ref.at[:, low_sib, edge], got_corner, sems, 0, sib)
    swap_low = remote(acc_ref.at[:, low_sib, body], got_low, sems, 1, sib)
    swap_edge = remote(acc_ref.at[:, top_sib, edge], got_edge, sems, 2, sib)
    swap_top = remote(acc_ref.at[:, top_sib, body], got_top, sems, 3, sib)

    @pl.when(has_right & has_down)
    def _():
        swap_corner.start()

    @pl.when(has_down)
    def _():
        swap_low.start()

    @pl.when(has_right)
    def _():
        swap_edge.start()

    swap_top.start()

    def part(src, dst, rows, cols, slot, where):
        return remote(src.at[:, rows, cols], dst.at[:, rows, cols], sems, slot, where)

    corner_near = part(right_corner, left_corner, near_rows, first, 4, right)
    corner_far = part(right_corner, left_corner, far_rows, first, 5, right)
    side = remote(right_edge, left_edge, sems, 6, right)
    rest_near = part(to_down, from_up, near_rows, rest, 7, down)
    rest_far = part(to_down, from_up, far_rows, rest, 8, down)
    first_near = part(to_down, from_up, near_rows, first, 9, down)
    first_far = part(to_down, from_up, far_rows, first, 10, down)

    def both(near_copy, far_copy, act):
        act(near_copy)

        @pl.when(whole)
        def _():
            act(far_copy)

    start, recv, sent = (lambda x: x.start()), (lambda x: x.wait_recv()), (lambda x: x.wait_send())

    if with_probe:
        own = chip(r, c)
        base = m * sum_rows
        swap_sum.wait_recv()
        scatter = []
        for k, (row, col) in enumerate(places):
            value = sum_ref[:, rows_of(row, col, base), :] + got_sum[:, rows_of(row, col), :]
            give[k] = encode(value)
            scatter.append(remote(give.at[k], gotten.at[k], psems, 1 + k, peers[k]))
            scatter[-1].start()

    @pl.when(has_right & has_down)
    def _():
        swap_corner.wait_recv()
        right_corner[...] = (acc_ref[:, low_mine, edge] + got_corner[...]).astype(BF16)
        both(corner_near, corner_far, start)

    @pl.when(has_down)
    def _():
        swap_low.wait_recv()
        to_down[:, :, rest] = (acc_ref[:, low_mine, rest] + got_low[:, :, rest]).astype(BF16)
        both(rest_near, rest_far, start)
        low_left[...] = acc_ref[:, low_mine, first] + got_low[:, :, first]

    @pl.when(has_right)
    def _():
        swap_edge.wait_recv()
        right_edge[...] = (acc_ref[:, top_mine, edge] + got_edge[...]).astype(BF16)
        side.start()

    swap_top.wait_recv()
    total[...] = acc_ref[:, top_mine, body] + got_top[...]
    peak = probe_ref[0] * probe_ref[0] + probe_ref[1] * probe_ref[1]
    peak = jnp.max(peak, keepdims=True) + EPSILON

    @pl.when(has_left & has_down)
    def _():
        corner_near.wait_recv()
        low_left[:, near_rows, :] += left_corner[:, near_rows, :].astype(F32)

        @pl.when(whole)
        def _():
            corner_far.wait_recv()
            low_left[:, far_rows, :] += left_corner[:, far_rows, :].astype(F32)

    @pl.when(has_down)
    def _():
        to_down[:, :, first] = low_left[...].astype(BF16)
        both(first_near, first_far, start)

    if with_probe:
        value = sum_ref[:, rows_of(r, c, base), :] + got_sum[:, rows_of(r, c), :]
        for k in range(len(steps)):
            scatter[k].wait_recv()
            value = value + decode(gotten[k])
        weight = value[2:] + REGULARIZER
        mine_code[own] = encode(value[:2] / weight)
        spread, crossings = [], []
        for k in range(len(steps)):
            spread.append(remote(mine_code.at[own], mine_code.at[own], asems, k, peers[k]))
            spread[-1].start()
        crossings.append(remote(mine_code.at[own], sib_code.at[own], fsems, 0, sib))
        crossings[0].start()
    else:
        out_ref[...] = jnp.zeros_like(out_ref)

    @pl.when(has_left)
    def _():
        side.wait_recv()
        total[:, :, first] += left_edge[...].astype(F32)

    @pl.when(has_up)
    def _():
        rest_near.wait_recv()
        first_near.wait_recv()
        total[:, near_rows, :] += from_up[:, near_rows, :].astype(F32)

        @pl.when(whole)
        def _():
            rest_far.wait_recv()
            first_far.wait_recv()
            total[:, far_rows, :] += from_up[:, far_rows, :].astype(F32)

    for plane in range(2):
        share_ref[:, plane, :] = field_ref[top_mine, plane, :] + total[plane] / peak

    if with_probe:

        def finish(codes, row, col, base):
            rows = rows_of(row, col, base)
            fresh = probe_ref[:, rows, :] + decode(codes[chip(row, col)])
            for plane in range(2):
                out_ref[rows, plane, :] = fresh[plane]

        origins = [(lax.rem(r + rows_n - a, rows_n), lax.rem(c + cols_n - b, cols_n)) for a, b in steps]
        for k, (row, col) in enumerate(origins):
            spread[k].wait_recv()
            at = chip(row, col)
            crossings.append(remote(mine_code.at[at], sib_code.at[at], fsems, 1 + k, sib))
            crossings[-1].start()
        for row, col in [(r, c)] + origins:
            finish(mine_code, row, col, base)
        for k, (row, col) in enumerate([(r, c)] + origins):
            crossings[k].wait_recv()
            finish(sib_code, row, col, sum_rows - base)

    swap_top.wait_send()

    @pl.when(has_right)
    def _():
        swap_edge.wait_send()
        side.wait_send()

    @pl.when(has_down)
    def _():
        swap_low.wait_send()
        both(rest_near, rest_far, sent)
        both(first_near, first_far, sent)

    @pl.when(has_right & has_down)
    def _():
        swap_corner.wait_send()
        both(corner_near, corner_far, sent)

    if with_probe:
        swap_sum.wait_send()
        for copy in scatter + spread + crossings:
            copy.wait_send()


def merge(acc, sums, probe, field, rows_n, cols_n, with_probe):
    tile_r, _, tile_c = field.shape
    frame = probe.shape[1]
    half = tile_r // 2
    sum_rows = frame // 2
    chips = rows_n * cols_n if with_probe else 2
    shard = sum_rows // chips if with_probe else 16
    in_vmem = pl.BlockSpec(memory_space=VMEM)
    return pl.pallas_call(
        functools.partial(merge_kernel, rows_n, cols_n, with_probe),
        out_shape=(
            jax.ShapeDtypeStruct((half, 2, tile_c), F32),
            jax.ShapeDtypeStruct((frame, 2, frame), F32),
        ),
        in_specs=[in_vmem] * 4,
        out_specs=(in_vmem, in_vmem),
        scratch_shapes=[
            VMEM((2, half, frame), F32),
            VMEM((2, half, tile_c), F32),
            VMEM((2, half, frame), F32),
            VMEM((2, half, tile_c), F32),
            VMEM((2, half, tile_c), F32),
            VMEM((2, half, frame), F32),
            VMEM((2, half, frame), BF16),
            VMEM((2, half, frame), BF16),
            VMEM((2, half, frame), BF16),
            VMEM((2, half, frame), BF16),
            VMEM((2, half, tile_c), BF16),
            VMEM((2, half, tile_c), BF16),
            VMEM((3, sum_rows, frame), F32),
            VMEM((chips - 1, 3, shard, frame), jnp.int16),
            VMEM((chips - 1, 3, shard, frame), jnp.int16),
            VMEM((chips, 2, shard, frame), jnp.int16),
            VMEM((chips, 2, shard, frame), jnp.int16),
            pltpu.SemaphoreType.DMA((2, 11)),
            pltpu.SemaphoreType.DMA((2, chips)),
            pltpu.SemaphoreType.DMA((2, chips)),
            pltpu.SemaphoreType.DMA((2, chips)),
        ],
        compiler_params=pltpu.CompilerParams(
            collective_id=1, has_side_effects=True, vmem_limit_bytes=16 << 20
        ),
        name="merge",
    )(acc, sums, probe, field)


def store_kernel(share_ref, fresh_ref, share_hbm, fresh_hbm, sems):
    pairs = [(share_ref, share_hbm), (fresh_ref, fresh_hbm)]
    copies = [pltpu.make_async_copy(a, b, sems.at[i]) for i, (a, b) in enumerate(pairs)]
    for copy in copies:
        copy.start()
    for copy in copies:
        copy.wait()


def store(share, fresh):
    return pl.pallas_call(
        store_kernel,
        out_shape=tuple(jax.ShapeDtypeStruct(x.shape, x.dtype) for x in (share, fresh)),
        in_specs=[pl.BlockSpec(memory_space=VMEM)] * 2,
        out_specs=(pl.BlockSpec(memory_space=pltpu.HBM),) * 2,
        scratch_shapes=[pltpu.SemaphoreType.DMA((2,))],
        compiler_params=pltpu.CompilerParams(vmem_limit_bytes=1 << 20),
        name="store",
    )(share, fresh)


def body(rows_n, cols_n, object_field, probe_field, amplitudes, row_offset, col_offset, counts):
    frame = probe_field.shape[0]
    first, second = dft_tables(frame)
    extras = (row_offset, col_offset, amplitudes, first, second)
    obj, probe, acc, *extras = halo(object_field, probe_field, extras, rows_n, cols_n)
    rows, cols, amplitudes, first, second = extras
    acc, sums = frames(rows, cols, counts, obj, probe, amplitudes, first, second, acc)
    with_probe = frame % (2 * rows_n * cols_n * 16) == 0
    object_new, fresh = merge(acc, sums, probe, object_field, rows_n, cols_n, with_probe)
    if not with_probe:
        sums = lax.psum(sums, ("row", "col", "mode"))
        fresh = probe + sums[:2] / (sums[2:] + REGULARIZER)
        fresh = jnp.moveaxis(fresh, 0, 1)
    return store(object_new, fresh)


def solution(mesh):
    split = ("groups", "row", "col", "mode")
    placed = (
        P(("groups", "row"), None, "col"),
        P("groups", None, None),
        P(split, None, None),
        P(split),
        P(split),
        P(split),
    )
    return jax.shard_map(
        functools.partial(body, mesh.shape["row"], mesh.shape["col"]),
        mesh=mesh,
        in_specs=placed,
        out_specs=(P(("groups", "row", "mode"), None, "col"), P("groups", None, None)),
        check_vma=False,
    )
```

```python
import functools
import math

import jax
import jax.numpy as jnp
import numpy as np
from jax import lax
from jax.experimental import pallas as pl
from jax.experimental.pallas import tpu as pltpu
from jax.sharding import PartitionSpec as P

FLOOR_SQUARED = 0.25
EPSILON = 1e-05
REGULARIZER = 1.0
F32 = jnp.float32
BF16 = jnp.bfloat16
MESH = pl.DeviceIdType.MESH
VMEM = pltpu.VMEM
LANES = 128
SHIFT = 64
CODE_BITS = 14
CODE_BIAS = 120
PIECE = 32
AHEAD = 2


def dft_tables(points):
    index = np.arange(points)
    product = (index[:, None] * index[None, :]) % points
    angle = (2.0 * math.pi / points) * product.astype(np.float32)
    norm = np.float32(1.0 / math.sqrt(points))
    cosine = (np.cos(angle.astype(np.float32)) * norm).astype(np.float32)
    sine = (np.sin(angle.astype(np.float32)) * norm).astype(np.float32)
    first = np.block([[cosine, sine], [-sine, cosine]])
    second = np.block([[cosine, -sine], [sine, cosine]])
    return jnp.asarray(first, BF16), jnp.asarray(second, BF16)


def greet(peers):
    barrier = pltpu.get_barrier_semaphore()
    expected = jnp.int32(0)
    for present, where in peers:
        expected = expected + present.astype(jnp.int32)

        @pl.when(present)
        def _(where=where):
            pl.semaphore_signal(barrier, inc=1, device_id=where, device_id_type=MESH)

    return expected


def remote(src, dst, sems, slot, where):
    return pltpu.make_async_remote_copy(
        src_ref=src,
        dst_ref=dst,
        send_sem=sems.at[0, slot],
        recv_sem=sems.at[1, slot],
        device_id=where,
        device_id_type=MESH,
    )


def halo_kernel(rows_n, cols_n, count, *refs):
    field_hbm, probe_hbm = refs[:2]
    extras = refs[2 : 2 + count]
    obj_ref, planes_ref, acc_ref = refs[2 + count : 5 + count]
    landed = refs[5 + count : 5 + 2 * count]
    field_ref, probe_ref, sems, local = refs[5 + 2 * count :]
    r = lax.axis_index("row")
    c = lax.axis_index("col")
    m = lax.axis_index("mode")
    tile_r, _, tile_c = field_ref.shape
    frame = probe_ref.shape[0]
    half, reach = tile_r // 2, frame - SHIFT
    low = reach // 2
    chunks = tile_r // PIECE
    strips = [
        pl.ds(pl.multiple_of(lax.rem(m * (low // PIECE) + k, chunks) * PIECE, PIECE), PIECE)
        for k in range(chunks)
    ]
    pairs = [(field_hbm.at[strip], field_ref.at[strip]) for strip in strips]
    pairs += [(probe_hbm, probe_ref), *zip(extras, landed)]
    fetches = [pltpu.make_async_copy(a, b, local.at[i]) for i, (a, b) in enumerate(pairs)]
    for fetch in fetches[:chunks]:
        fetch.start()
    has_up, has_down = r > 0, r < rows_n - 1
    has_left, has_right = c > 0, c < cols_n - 1
    sib = {"mode": 1 - m}
    up, down = {"row": r - 1}, {"row": r + 1}
    left, right = {"col": c - 1}, {"col": c + 1}
    always = m >= 0
    peers = [(always, sib), (has_up, up), (has_down, down), (has_left, left), (has_right, right)]
    expected = greet(peers)
    mine = pl.ds(pl.multiple_of(m * half, half), half)
    lift = pl.ds(pl.multiple_of(m * low, 32), low)
    below = pl.ds(pl.multiple_of(tile_r + m * low, 32), low)
    first, rest, edge = pl.ds(0, frame), pl.ds(frame, tile_c - frame), pl.ds(tile_c, frame)

    def part(rows, cols, to_rows, to_cols, slot, where):
        return remote(
            obj_ref.at[:, rows, cols], obj_ref.at[:, to_rows, to_cols], sems, slot, where
        )

    pieces = [pl.ds(pl.multiple_of(m * low + k, PIECE), PIECE) for k in range(0, low, PIECE)]
    landing = [
        pl.ds(pl.multiple_of(tile_r + m * low + k, PIECE), PIECE) for k in range(0, low, PIECE)
    ]
    n = len(pieces)
    up_first = [part(a, first, b, first, k, up) for k, (a, b) in enumerate(zip(pieces, landing))]
    corner = [part(b, first, b, edge, n + k, left) for k, b in enumerate(landing)]
    swap_corner = [part(b, edge, b, edge, 2 * n + k, sib) for k, b in enumerate(landing)]
    to_left = part(mine, first, mine, edge, 3 * n, left)
    up_rest = part(lift, rest, below, rest, 3 * n + 1, up)
    swap_edge = part(mine, edge, mine, edge, 3 * n + 2, sib)
    swap_first = part(below, first, below, first, 3 * n + 3, sib)
    swap_rest = part(below, rest, below, rest, 3 * n + 4, sib)

    def convert(k):
        fetches[k].wait()
        for plane in range(2):
            obj_ref[plane, strips[k], :tile_c] = field_ref[strips[k], plane, :].astype(BF16)

    for k in range(n):
        convert(k)
        if k == 0:
            pl.semaphore_wait(pltpu.get_barrier_semaphore(), expected)

        @pl.when(has_up)
        def _(k=k):
            up_first[k].start()

    for fetch in fetches[chunks:]:
        fetch.start()
    enough = (tile_r - low) // PIECE
    for k in range(n, enough):
        convert(k)

    @pl.when(has_left)
    def _():
        to_left.start()

    for k in range(enough, chunks):
        convert(k)
    fetches[chunks].wait()
    for plane in range(2):
        planes_ref[plane] = probe_ref[:, plane, :]
    acc_ref[...] = jnp.zeros(acc_ref.shape, F32)

    @pl.when(has_up)
    def _():
        for copy in up_first[:AHEAD]:
            copy.wait_send()
        up_rest.start()

    @pl.when(has_down)
    def _():
        for k in range(n):
            up_first[k].wait_recv()

            @pl.when(has_left)
            def _(k=k):
                corner[k].start()

        swap_first.start()

    @pl.when(has_right)
    def _():
        to_left.wait_recv()
        swap_edge.start()

    def turn(k):
        @pl.when(has_right & has_down)
        def _():
            corner[k].wait_recv()
            swap_corner[k].start()

    turn(0)

    @pl.when(has_down)
    def _():
        up_rest.wait_recv()
        swap_rest.start()

    for k in range(1, n):
        turn(k)

    @pl.when(has_right)
    def _():
        swap_edge.wait()

    @pl.when(has_down)
    def _():
        swap_first.wait()
        swap_rest.wait()

        @pl.when(has_left)
        def _():
            for copy in corner:
                copy.wait_send()

    @pl.when(has_left)
    def _():
        to_left.wait_send()

    @pl.when(has_up)
    def _():
        for copy in up_first[AHEAD:]:
            copy.wait_send()
        up_rest.wait_send()

    @pl.when(has_right & has_down)
    def _():
        for copy in swap_corner:
            copy.wait()

    for fetch in fetches[chunks + 1 :]:
        fetch.wait()


def halo(field, probe, extras, rows_n, cols_n):
    tile_r, planes, tile_c = field.shape
    frame = probe.shape[0]
    shape = (planes, tile_r + frame, tile_c + frame)
    in_vmem = pl.BlockSpec(memory_space=VMEM)
    return pl.pallas_call(
        functools.partial(halo_kernel, rows_n, cols_n, len(extras)),
        out_shape=(
            jax.ShapeDtypeStruct(shape, BF16),
            jax.ShapeDtypeStruct((planes, frame, frame), F32),
            jax.ShapeDtypeStruct(shape, F32),
            *(jax.ShapeDtypeStruct(x.shape, x.dtype) for x in extras),
        ),
        in_specs=[pl.BlockSpec(memory_space=pltpu.HBM)] * (2 + len(extras)),
        out_specs=(in_vmem,) * (3 + len(extras)),
        scratch_shapes=[
            VMEM(field.shape, F32),
            VMEM(probe.shape, F32),
            pltpu.SemaphoreType.DMA((2, 5 + 3 * ((frame - SHIFT) // 2 // PIECE))),
            pltpu.SemaphoreType.DMA((tile_r // PIECE + 1 + len(extras),)),
        ],
        cost_estimate=pl.CostEstimate(flops=0, bytes_accessed=40 << 20, transcendentals=0),
        compiler_params=pltpu.CompilerParams(
            collective_id=0, has_side_effects=True, vmem_limit_bytes=8 << 20
        ),
        name="halo",
    )(*(pltpu.with_memory_space_constraint(x, pltpu.HBM) for x in (field, probe, *extras)))


def frames_kernel(
    row_ref, col_ref, count_ref, obj, probe_ref, amp_ref, first_ref, second_ref, _zero,
    acc, sum_ref, patch, tall, wide, field,
):
    frame = probe_ref.shape[1]
    ext_rows, ext_cols = obj.shape[1:]
    top = lax.axis_index("row") * (ext_rows - frame)
    left = lax.axis_index("col") * (ext_cols - frame)
    step = 32
    chunks = range(0, frame, step)
    tiles = frame // LANES
    lane = lax.broadcasted_iota(jnp.int32, (step, LANES), 1)
    sum_ref[...] = jnp.zeros_like(sum_ref)

    def place(slot):
        row = row_ref[slot] - top
        col = col_ref[slot] - left
        return row, (col // LANES) * LANES, col % LANES

    def columns(base, tile):
        return pl.ds(pl.multiple_of(base + tile * LANES, LANES), LANES)

    def enter(slot, at):
        row, base, shift = place(slot)
        for k in chunks:
            rows = pl.ds(pl.multiple_of(row + k, step), step)
            here = pl.ds(k, step)
            for plane in range(2):
                turned = []
                for tile in range(tiles + 1):
                    value = obj[plane, rows, columns(base, tile)].astype(F32)
                    turned.append(pltpu.roll(value, shift, 1))
                for tile in range(tiles):
                    value = jnp.where(lane < LANES - shift, turned[tile], turned[tile + 1])
                    patch[at, plane, here, tile * LANES : (tile + 1) * LANES] = value.astype(BF16)
            o_re, o_im = patch[at, 0, here, :].astype(F32), patch[at, 1, here, :].astype(F32)
            p_re, p_im = probe_ref[0, here, :], probe_ref[1, here, :]
            tall[at, here, :] = (p_re * o_re - p_im * o_im).astype(BF16)
            tall[at, frame + k : frame + k + step, :] = (p_re * o_im + p_im * o_re).astype(BF16)

    def transform(at, one_ref, two_ref):
        half = jnp.dot(one_ref[...], tall[at], preferred_element_type=F32).astype(BF16)
        wide[at, :, :frame] = half[:frame]
        wide[at, :, frame:] = half[frame:]
        field[at] = jnp.dot(wide[at], two_ref[...], preferred_element_type=F32)

    def constrain(slot, at):
        for k in chunks:
            here = pl.ds(k, step)
            f_re = field[at, here, :frame]
            f_im = field[at, here, frame:]
            amp = amp_ref[slot, here, :].astype(F32)
            power = f_re * f_re + f_im * f_im
            factor = amp * lax.rsqrt(jnp.maximum(power, FLOOR_SQUARED)) - 1.0
            tall[at, here, :] = (f_re * factor).astype(BF16)
            tall[at, frame + k : frame + k + step, :] = (f_im * factor).astype(BF16)

    def leave(slot, at):
        row, base, shift = place(slot)
        for k in chunks:
            rows = pl.ds(pl.multiple_of(row + k, step), step)
            here = pl.ds(k, step)
            x_re = field[at, here, :frame]
            x_im = field[at, here, frame:]
            p_re, p_im = probe_ref[0, here, :], probe_ref[1, here, :]
            o_re, o_im = patch[at, 0, here, :].astype(F32), patch[at, 1, here, :].astype(F32)
            for plane, value in enumerate((p_re * x_re + p_im * x_im, p_re * x_im - p_im * x_re)):
                turned = [
                    pltpu.roll(value[:, t * LANES : (t + 1) * LANES], shift, 1) for t in range(tiles)
                ]
                for tile in range(tiles + 1):
                    if tile == 0:
                        part = jnp.where(lane >= shift, turned[0], 0.0)
                    elif tile == tiles:
                        part = jnp.where(lane < shift, turned[-1], 0.0)
                    else:
                        part = jnp.where(lane < shift, turned[tile - 1], turned[tile])
                    acc[plane, rows, columns(base, tile)] += part
            sum_ref[0, here, :] += o_re * x_re + o_im * x_im
            sum_ref[1, here, :] += o_re * x_im - o_im * x_re
            sum_ref[2, here, :] += o_re * o_re + o_im * o_im

    def run(slots):
        for at, slot in enumerate(slots):
            enter(slot, at)
            transform(at, first_ref, second_ref)
        for at, slot in enumerate(slots):
            constrain(slot, at)
            transform(at, second_ref, first_ref)
        for at, slot in enumerate(slots):
            leave(slot, at)

    def choice(live):
        @pl.when(count_ref[0] == live)
        def _():
            run(range(live))

    for live in range(1, amp_ref.shape[0] + 1):
        choice(live)


def frames(row_offset, col_offset, counts, obj, probe, amplitudes, first, second, acc):
    frame = probe.shape[1]
    slots = amplitudes.shape[0]
    in_vmem = pl.BlockSpec(memory_space=VMEM)
    in_smem = pl.BlockSpec(memory_space=pltpu.SMEM)
    return pl.pallas_call(
        frames_kernel,
        out_shape=(
            jax.ShapeDtypeStruct(acc.shape, F32),
            jax.ShapeDtypeStruct((3, frame, frame), F32),
        ),
        in_specs=[in_smem] * 3 + [in_vmem] * 6,
        out_specs=(in_vmem, in_vmem),
        input_output_aliases={8: 0},
        scratch_shapes=[
            VMEM((slots, 2, frame, frame), BF16),
            VMEM((slots, 2 * frame, frame), BF16),
            VMEM((slots, frame, 2 * frame), BF16),
            VMEM((slots, frame, 2 * frame), F32),
        ],
        compiler_params=pltpu.CompilerParams(vmem_limit_bytes=14 << 20),
        name="frames",
    )(row_offset, col_offset, counts, obj, probe, amplitudes, first, second, acc)


def encode(value):
    rows = lax.broadcasted_iota(jnp.int32, value.shape, value.ndim - 2)
    peak = jnp.max(jnp.abs(value), axis=-2, keepdims=True)
    power = jnp.ceil(jnp.log2(jnp.maximum(peak, 1e-30)) + 0.01)
    bits = (power.astype(jnp.int32) + CODE_BIAS) >> (rows % 8)
    whole = jnp.round(value * jnp.exp2(CODE_BITS - power)).astype(jnp.int32)
    return (2 * whole + (bits & 1)).astype(jnp.int16)


def decode(code):
    code = code.astype(jnp.int32)
    rows = lax.broadcasted_iota(jnp.int32, code.shape, code.ndim - 2)
    low = code & 1
    bits = jnp.where(rows < 8, low << (rows % 8), 0)
    power = jnp.sum(bits, axis=-2, keepdims=True) - CODE_BIAS
    return (code - low).astype(F32) * jnp.exp2(power.astype(F32) - (CODE_BITS + 1))


def merge_kernel(
    rows_n, cols_n, with_probe, acc_ref, sum_ref, probe_ref, field_ref, share_ref, out_ref,
    got_corner, got_low, got_edge, got_top, total, low_left,
    right_corner, left_corner, right_edge, left_edge, to_down, from_up,
    got_sum, give, gotten, mine_code, sib_code, sems, psems, asems, fsems,
):
    r = lax.axis_index("row")
    c = lax.axis_index("col")
    m = lax.axis_index("mode")
    half, _, tile_c = share_ref.shape
    tile_r = 2 * half
    frame = probe_ref.shape[1]
    near = frame - SHIFT - half
    has_up, has_down = r > 0, r < rows_n - 1
    has_left, has_right = c > 0, c < cols_n - 1
    whole = m == 0
    sib = {"mode": 1 - m}
    up, down = {"row": r - 1}, {"row": r + 1}
    left, right = {"col": c - 1}, {"col": c + 1}
    always = m >= 0
    steps = [(a, b) for a in range(rows_n) for b in range(cols_n) if a or b]
    places = [(lax.rem(r + a, rows_n), lax.rem(c + b, cols_n)) for a, b in steps]
    peers = [{"row": a, "col": b} for a, b in places]
    if with_probe:
        expected = greet([(always, p) for p in [sib] + peers])
    else:
        near_by = [(has_up, up), (has_down, down), (has_left, left), (has_right, right)]
        expected = greet([(always, sib)] + near_by)
    pl.semaphore_wait(pltpu.get_barrier_semaphore(), expected)

    def block(which, base):
        return pl.ds(pl.multiple_of(which * half + base, half), half)

    top_mine, low_mine = block(m, 0), block(m, tile_r)
    top_sib, low_sib = block(1 - m, 0), block(1 - m, tile_r)
    body, edge = pl.ds(0, tile_c), pl.ds(tile_c, frame)
    first, rest = pl.ds(0, frame), pl.ds(frame, tile_c - frame)
    near_rows, far_rows = pl.ds(0, near), pl.ds(near, half - near)
    sum_rows = frame // 2
    shard = sum_rows // (rows_n * cols_n)

    def chip(row, col):
        return row * cols_n + col

    def rows_of(row, col, base=0):
        return pl.ds(pl.multiple_of(base + chip(row, col) * shard, shard), shard)

    if with_probe:
        away = pl.ds(pl.multiple_of((1 - m) * sum_rows, sum_rows), sum_rows)
        swap_sum = remote(sum_ref.at[:, away, :], got_sum, psems, 0, sib)
        swap_sum.start()
    swap_corner = remote(acc_ref.at[:, low_sib, edge], got_corner, sems, 0, sib)
    swap_low = remote(acc_ref.at[:, low_sib, body], got_low, sems, 1, sib)
    swap_edge = remote(acc_ref.at[:, top_sib, edge], got_edge, sems, 2, sib)
    swap_top = remote(acc_ref.at[:, top_sib, body], got_top, sems, 3, sib)

    @pl.when(has_right & has_down)
    def _():
        swap_corner.start()

    @pl.when(has_down)
    def _():
        swap_low.start()

    @pl.when(has_right)
    def _():
        swap_edge.start()

    swap_top.start()

    def part(src, dst, rows, cols, slot, where):
        return remote(src.at[:, rows, cols], dst.at[:, rows, cols], sems, slot, where)

    corner_near = part(right_corner, left_corner, near_rows, first, 4, right)
    corner_far = part(right_corner, left_corner, far_rows, first, 5, right)
    side = remote(right_edge, left_edge, sems, 6, right)
    rest_near = part(to_down, from_up, near_rows, rest, 7, down)
    rest_far = part(to_down, from_up, far_rows, rest, 8, down)
    first_near = part(to_down, from_up, near_rows, first, 9, down)
    first_far = part(to_down, from_up, far_rows, first, 10, down)

    def both(near_copy, far_copy, act):
        act(near_copy)

        @pl.when(whole)
        def _():
            act(far_copy)

    start, recv, sent = (lambda x: x.start()), (lambda x: x.wait_recv()), (lambda x: x.wait_send())

    if with_probe:
        own = chip(r, c)
        base = m * sum_rows
        swap_sum.wait_recv()
        scatter = []
        for k, (row, col) in enumerate(places):
            value = sum_ref[:, rows_of(row, col, base), :] + got_sum[:, rows_of(row, col), :]
            give[k] = encode(value)
            scatter.append(remote(give.at[k], gotten.at[k], psems, 1 + k, peers[k]))
            scatter[-1].start()

    @pl.when(has_right & has_down)
    def _():
        swap_corner.wait_recv()
        right_corner[...] = (acc_ref[:, low_mine, edge] + got_corner[...]).astype(BF16)
        both(corner_near, corner_far, start)

    @pl.when(has_down)
    def _():
        swap_low.wait_recv()
        to_down[:, :, rest] = (acc_ref[:, low_mine, rest] + got_low[:, :, rest]).astype(BF16)
        both(rest_near, rest_far, start)
        low_left[...] = acc_ref[:, low_mine, first] + got_low[:, :, first]

    @pl.when(has_right)
    def _():
        swap_edge.wait_recv()
        right_edge[...] = (acc_ref[:, top_mine, edge] + got_edge[...]).astype(BF16)
        side.start()

    swap_top.wait_recv()
    total[...] = acc_ref[:, top_mine, body] + got_top[...]
    peak = probe_ref[0] * probe_ref[0] + probe_ref[1] * probe_ref[1]
    peak = jnp.max(peak, keepdims=True) + EPSILON

    @pl.when(has_left & has_down)
    def _():
        corner_near.wait_recv()
        low_left[:, near_rows, :] += left_corner[:, near_rows, :].astype(F32)

        @pl.when(whole)
        def _():
            corner_far.wait_recv()
            low_left[:, far_rows, :] += left_corner[:, far_rows, :].astype(F32)

    @pl.when(has_down)
    def _():
        to_down[:, :, first] = low_left[...].astype(BF16)
        both(first_near, first_far, start)

    if with_probe:
        value = sum_ref[:, rows_of(r, c, base), :] + got_sum[:, rows_of(r, c), :]
        for k in range(len(steps)):
            scatter[k].wait_recv()
            value = value + decode(gotten[k])
        weight = value[2:] + REGULARIZER
        mine_code[own] = encode(value[:2] / weight)
        spread, crossings = [], []
        for k in range(len(steps)):
            spread.append(remote(mine_code.at[own], mine_code.at[own], asems, k, peers[k]))
            spread[-1].start()
        crossings.append(remote(mine_code.at[own], sib_code.at[own], fsems, 0, sib))
        crossings[0].start()
    else:
        out_ref[...] = jnp.zeros_like(out_ref)

    @pl.when(has_left)
    def _():
        side.wait_recv()
        total[:, :, first] += left_edge[...].astype(F32)

    @pl.when(has_up)
    def _():
        rest_near.wait_recv()
        first_near.wait_recv()
        total[:, near_rows, :] += from_up[:, near_rows, :].astype(F32)

        @pl.when(whole)
        def _():
            rest_far.wait_recv()
            first_far.wait_recv()
            total[:, far_rows, :] += from_up[:, far_rows, :].astype(F32)

    for plane in range(2):
        share_ref[:, plane, :] = field_ref[top_mine, plane, :] + total[plane] / peak

    if with_probe:

        def finish(codes, row, col, base):
            rows = rows_of(row, col, base)
            fresh = probe_ref[:, rows, :] + decode(codes[chip(row, col)])
            for plane in range(2):
                out_ref[rows, plane, :] = fresh[plane]

        origins = [(lax.rem(r + rows_n - a, rows_n), lax.rem(c + cols_n - b, cols_n)) for a, b in steps]
        for k, (row, col) in enumerate(origins):
            spread[k].wait_recv()
            at = chip(row, col)
            crossings.append(remote(mine_code.at[at], sib_code.at[at], fsems, 1 + k, sib))
            crossings[-1].start()
        for row, col in [(r, c)] + origins:
            finish(mine_code, row, col, base)
        for k, (row, col) in enumerate([(r, c)] + origins):
            crossings[k].wait_recv()
            finish(sib_code, row, col, sum_rows - base)

    swap_top.wait_send()

    @pl.when(has_right)
    def _():
        swap_edge.wait_send()
        side.wait_send()

    @pl.when(has_down)
    def _():
        swap_low.wait_send()
        both(rest_near, rest_far, sent)
        both(first_near, first_far, sent)

    @pl.when(has_right & has_down)
    def _():
        swap_corner.wait_send()
        both(corner_near, corner_far, sent)

    if with_probe:
        swap_sum.wait_send()
        for copy in scatter + spread + crossings:
            copy.wait_send()


def merge(acc, sums, probe, field, rows_n, cols_n, with_probe):
    tile_r, _, tile_c = field.shape
    frame = probe.shape[1]
    half = tile_r // 2
    sum_rows = frame // 2
    chips = rows_n * cols_n if with_probe else 2
    shard = sum_rows // chips if with_probe else 16
    in_vmem = pl.BlockSpec(memory_space=VMEM)
    return pl.pallas_call(
        functools.partial(merge_kernel, rows_n, cols_n, with_probe),
        out_shape=(
            jax.ShapeDtypeStruct((half, 2, tile_c), F32),
            jax.ShapeDtypeStruct((frame, 2, frame), F32),
        ),
        in_specs=[in_vmem] * 4,
        out_specs=(in_vmem, in_vmem),
        scratch_shapes=[
            VMEM((2, half, frame), F32),
            VMEM((2, half, tile_c), F32),
            VMEM((2, half, frame), F32),
            VMEM((2, half, tile_c), F32),
            VMEM((2, half, tile_c), F32),
            VMEM((2, half, frame), F32),
            VMEM((2, half, frame), BF16),
            VMEM((2, half, frame), BF16),
            VMEM((2, half, frame), BF16),
            VMEM((2, half, frame), BF16),
            VMEM((2, half, tile_c), BF16),
            VMEM((2, half, tile_c), BF16),
            VMEM((3, sum_rows, frame), F32),
            VMEM((chips - 1, 3, shard, frame), jnp.int16),
            VMEM((chips - 1, 3, shard, frame), jnp.int16),
            VMEM((chips, 2, shard, frame), jnp.int16),
            VMEM((chips, 2, shard, frame), jnp.int16),
            pltpu.SemaphoreType.DMA((2, 11)),
            pltpu.SemaphoreType.DMA((2, chips)),
            pltpu.SemaphoreType.DMA((2, chips)),
            pltpu.SemaphoreType.DMA((2, chips)),
        ],
        compiler_params=pltpu.CompilerParams(
            collective_id=1, has_side_effects=True, vmem_limit_bytes=16 << 20
        ),
        name="merge",
    )(acc, sums, probe, field)


def store_kernel(share_ref, fresh_ref, share_hbm, fresh_hbm, sems):
    pairs = [(share_ref, share_hbm), (fresh_ref, fresh_hbm)]
    copies = [pltpu.make_async_copy(a, b, sems.at[i]) for i, (a, b) in enumerate(pairs)]
    for copy in copies:
        copy.start()
    for copy in copies:
        copy.wait()


def store(share, fresh):
    return pl.pallas_call(
        store_kernel,
        out_shape=tuple(jax.ShapeDtypeStruct(x.shape, x.dtype) for x in (share, fresh)),
        in_specs=[pl.BlockSpec(memory_space=VMEM)] * 2,
        out_specs=(pl.BlockSpec(memory_space=pltpu.HBM),) * 2,
        scratch_shapes=[pltpu.SemaphoreType.DMA((2,))],
        compiler_params=pltpu.CompilerParams(vmem_limit_bytes=1 << 20),
        name="store",
    )(share, fresh)


def body(rows_n, cols_n, object_field, probe_field, amplitudes, row_offset, col_offset, counts):
    frame = probe_field.shape[0]
    first, second = dft_tables(frame)
    extras = (row_offset, col_offset, amplitudes, first, second)
    obj, probe, acc, *extras = halo(object_field, probe_field, extras, rows_n, cols_n)
    rows, cols, amplitudes, first, second = extras
    acc, sums = frames(rows, cols, counts, obj, probe, amplitudes, first, second, acc)
    with_probe = frame % (2 * rows_n * cols_n * 16) == 0
    object_new, fresh = merge(acc, sums, probe, object_field, rows_n, cols_n, with_probe)
    if not with_probe:
        sums = lax.psum(sums, ("row", "col", "mode"))
        fresh = probe + sums[:2] / (sums[2:] + REGULARIZER)
        fresh = jnp.moveaxis(fresh, 0, 1)
    return store(object_new, fresh)


def solution(mesh):
    split = ("groups", "row", "col", "mode")
    placed = (
        P(("groups", "row"), None, "col"),
        P("groups", None, None),
        P(split, None, None),
        P(split),
        P(split),
        P(split),
    )
    return jax.shard_map(
        functools.partial(body, mesh.shape["row"], mesh.shape["col"]),
        mesh=mesh,
        in_specs=placed,
        out_specs=(P(("groups", "row", "mode"), None, "col"), P("groups", None, None)),
        check_vma=False,
    )
```

```python
import functools
import math

import jax
import jax.numpy as jnp
import numpy as np
from jax import lax
from jax.experimental import pallas as pl
from jax.experimental.pallas import tpu as pltpu
from jax.sharding import PartitionSpec as P

FLOOR_SQUARED = 0.25
EPSILON = 1e-05
REGULARIZER = 1.0
F32 = jnp.float32
BF16 = jnp.bfloat16
MESH = pl.DeviceIdType.MESH
VMEM = pltpu.VMEM
LANES = 128
SHIFT = 64
CODE_BITS = 14
CODE_BIAS = 120
PIECE = 32
AHEAD = 2
STEP = 16


def dft_tables(points):
    index = np.arange(points)
    product = (index[:, None] * index[None, :]) % points
    angle = (2.0 * math.pi / points) * product.astype(np.float32)
    norm = np.float32(1.0 / math.sqrt(points))
    cosine = (np.cos(angle.astype(np.float32)) * norm).astype(np.float32)
    sine = (np.sin(angle.astype(np.float32)) * norm).astype(np.float32)
    first = np.block([[cosine, sine], [-sine, cosine]])
    second = np.block([[cosine, -sine], [sine, cosine]])
    return jnp.asarray(first, BF16), jnp.asarray(second, BF16)


def greet(peers):
    barrier = pltpu.get_barrier_semaphore()
    expected = jnp.int32(0)
    for present, where in peers:
        expected = expected + present.astype(jnp.int32)

        @pl.when(present)
        def _(where=where):
            pl.semaphore_signal(barrier, inc=1, device_id=where, device_id_type=MESH)

    return expected


def remote(src, dst, sems, slot, where):
    return pltpu.make_async_remote_copy(
        src_ref=src,
        dst_ref=dst,
        send_sem=sems.at[0, slot],
        recv_sem=sems.at[1, slot],
        device_id=where,
        device_id_type=MESH,
    )


def halo_kernel(rows_n, cols_n, count, *refs):
    field_hbm, probe_hbm = refs[:2]
    extras = refs[2 : 2 + count]
    obj_ref, planes_ref, acc_ref = refs[2 + count : 5 + count]
    landed = refs[5 + count : 5 + 2 * count]
    field_ref, probe_ref, sems, local = refs[5 + 2 * count :]
    r = lax.axis_index("row")
    c = lax.axis_index("col")
    m = lax.axis_index("mode")
    tile_r, _, tile_c = field_ref.shape
    frame = probe_ref.shape[0]
    half, reach = tile_r // 2, frame - SHIFT
    low = reach // 2
    chunks = tile_r // PIECE
    strips = [
        pl.ds(pl.multiple_of(lax.rem(m * (low // PIECE) + k, chunks) * PIECE, PIECE), PIECE)
        for k in range(chunks)
    ]
    pairs = [(field_hbm.at[strip], field_ref.at[strip]) for strip in strips]
    pairs += [(probe_hbm, probe_ref), *zip(extras, landed)]
    fetches = [pltpu.make_async_copy(a, b, local.at[i]) for i, (a, b) in enumerate(pairs)]
    for fetch in fetches[:chunks]:
        fetch.start()
    has_up, has_down = r > 0, r < rows_n - 1
    has_left, has_right = c > 0, c < cols_n - 1
    sib = {"mode": 1 - m}
    up, down = {"row": r - 1}, {"row": r + 1}
    left, right = {"col": c - 1}, {"col": c + 1}
    always = m >= 0
    peers = [(always, sib), (has_up, up), (has_down, down), (has_left, left), (has_right, right)]
    expected = greet(peers)
    mine = pl.ds(pl.multiple_of(m * half, half), half)
    lift = pl.ds(pl.multiple_of(m * low, 32), low)
    below = pl.ds(pl.multiple_of(tile_r + m * low, 32), low)
    first, rest, edge = pl.ds(0, frame), pl.ds(frame, tile_c - frame), pl.ds(tile_c, frame)

    def part(rows, cols, to_rows, to_cols, slot, where):
        return remote(
            obj_ref.at[:, rows, cols], obj_ref.at[:, to_rows, to_cols], sems, slot, where
        )

    pieces = [pl.ds(pl.multiple_of(m * low + k, PIECE), PIECE) for k in range(0, low, PIECE)]
    landing = [
        pl.ds(pl.multiple_of(tile_r + m * low + k, PIECE), PIECE) for k in range(0, low, PIECE)
    ]
    n = len(pieces)
    up_first = [part(a, first, b, first, k, up) for k, (a, b) in enumerate(zip(pieces, landing))]
    corner = [part(b, first, b, edge, n + k, left) for k, b in enumerate(landing)]
    swap_corner = [part(b, edge, b, edge, 2 * n + k, sib) for k, b in enumerate(landing)]
    to_left = part(mine, first, mine, edge, 3 * n, left)
    up_rest = part(lift, rest, below, rest, 3 * n + 1, up)
    swap_edge = part(mine, edge, mine, edge, 3 * n + 2, sib)
    swap_first = part(below, first, below, first, 3 * n + 3, sib)
    swap_rest = part(below, rest, below, rest, 3 * n + 4, sib)

    def convert(k):
        fetches[k].wait()
        for plane in range(2):
            obj_ref[plane, strips[k], :tile_c] = field_ref[strips[k], plane, :].astype(BF16)

    for k in range(n):
        convert(k)
        if k == 0:
            pl.semaphore_wait(pltpu.get_barrier_semaphore(), expected)

        @pl.when(has_up)
        def _(k=k):
            up_first[k].start()

    for fetch in fetches[chunks:]:
        fetch.start()
    enough = (tile_r - low) // PIECE
    for k in range(n, enough):
        convert(k)

    @pl.when(has_left)
    def _():
        to_left.start()

    for k in range(enough, chunks):
        convert(k)
    fetches[chunks].wait()
    for plane in range(2):
        planes_ref[plane] = probe_ref[:, plane, :]
    acc_ref[...] = jnp.zeros(acc_ref.shape, F32)

    @pl.when(has_up)
    def _():
        for copy in up_first[:AHEAD]:
            copy.wait_send()
        up_rest.start()

    @pl.when(has_down)
    def _():
        for k in range(n):
            up_first[k].wait_recv()

            @pl.when(has_left)
            def _(k=k):
                corner[k].start()

        swap_first.start()

    @pl.when(has_right)
    def _():
        to_left.wait_recv()
        swap_edge.start()

    def turn(k):
        @pl.when(has_right & has_down)
        def _():
            corner[k].wait_recv()
            swap_corner[k].start()

    turn(0)

    @pl.when(has_down)
    def _():
        up_rest.wait_recv()
        swap_rest.start()

    for k in range(1, n):
        turn(k)

    @pl.when(has_right)
    def _():
        swap_edge.wait()

    @pl.when(has_down)
    def _():
        swap_first.wait()
        swap_rest.wait()

        @pl.when(has_left)
        def _():
            for copy in corner:
                copy.wait_send()

    @pl.when(has_left)
    def _():
        to_left.wait_send()

    @pl.when(has_up)
    def _():
        for copy in up_first[AHEAD:]:
            copy.wait_send()
        up_rest.wait_send()

    @pl.when(has_right & has_down)
    def _():
        for copy in swap_corner:
            copy.wait()

    for fetch in fetches[chunks + 1 :]:
        fetch.wait()


def halo(field, probe, extras, rows_n, cols_n):
    tile_r, planes, tile_c = field.shape
    frame = probe.shape[0]
    shape = (planes, tile_r + frame, tile_c + frame)
    in_vmem = pl.BlockSpec(memory_space=VMEM)
    return pl.pallas_call(
        functools.partial(halo_kernel, rows_n, cols_n, len(extras)),
        out_shape=(
            jax.ShapeDtypeStruct(shape, BF16),
            jax.ShapeDtypeStruct((planes, frame, frame), F32),
            jax.ShapeDtypeStruct(shape, F32),
            *(jax.ShapeDtypeStruct(x.shape, x.dtype) for x in extras),
        ),
        in_specs=[pl.BlockSpec(memory_space=pltpu.HBM)] * (2 + len(extras)),
        out_specs=(in_vmem,) * (3 + len(extras)),
        scratch_shapes=[
            VMEM(field.shape, F32),
            VMEM(probe.shape, F32),
            pltpu.SemaphoreType.DMA((2, 5 + 3 * ((frame - SHIFT) // 2 // PIECE))),
            pltpu.SemaphoreType.DMA((tile_r // PIECE + 1 + len(extras),)),
        ],
        cost_estimate=pl.CostEstimate(flops=0, bytes_accessed=40 << 20, transcendentals=0),
        compiler_params=pltpu.CompilerParams(
            collective_id=0, has_side_effects=True, vmem_limit_bytes=8 << 20
        ),
        name="halo",
    )(*(pltpu.with_memory_space_constraint(x, pltpu.HBM) for x in (field, probe, *extras)))


def frames_kernel(
    row_ref, col_ref, count_ref, obj, probe_ref, amp_ref, first_ref, second_ref, _zero,
    acc, field, patch, tall, wide,
):
    frame = probe_ref.shape[1]
    ext_rows, ext_cols = obj.shape[1:]
    top = lax.axis_index("row") * (ext_rows - frame)
    left = lax.axis_index("col") * (ext_cols - frame)
    step = 32
    chunks = range(0, frame, step)
    tiles = frame // LANES
    lane = lax.broadcasted_iota(jnp.int32, (step, LANES), 1)

    def place(slot):
        row = row_ref[slot] - top
        col = col_ref[slot] - left
        return row, (col // LANES) * LANES, col % LANES

    def columns(base, tile):
        return pl.ds(pl.multiple_of(base + tile * LANES, LANES), LANES)

    def enter(slot, at):
        row, base, shift = place(slot)
        for k in chunks:
            rows = pl.ds(pl.multiple_of(row + k, step), step)
            here = pl.ds(k, step)
            for plane in range(2):
                turned = []
                for tile in range(tiles + 1):
                    value = obj[plane, rows, columns(base, tile)].astype(F32)
                    turned.append(pltpu.roll(value, shift, 1))
                for tile in range(tiles):
                    value = jnp.where(lane < LANES - shift, turned[tile], turned[tile + 1])
                    patch[at, plane, here, tile * LANES : (tile + 1) * LANES] = value.astype(BF16)
            o_re, o_im = patch[at, 0, here, :].astype(F32), patch[at, 1, here, :].astype(F32)
            p_re, p_im = probe_ref[0, here, :], probe_ref[1, here, :]
            tall[at, here, :] = (p_re * o_re - p_im * o_im).astype(BF16)
            tall[at, frame + k : frame + k + step, :] = (p_re * o_im + p_im * o_re).astype(BF16)

    def transform(at, one_ref, two_ref):
        half = jnp.dot(one_ref[...], tall[at], preferred_element_type=F32).astype(BF16)
        wide[at, :, :frame] = half[:frame]
        wide[at, :, frame:] = half[frame:]
        field[at] = jnp.dot(wide[at], two_ref[...], preferred_element_type=F32)

    def constrain(slot, at):
        for k in chunks:
            here = pl.ds(k, step)
            f_re = field[at, here, :frame]
            f_im = field[at, here, frame:]
            amp = amp_ref[slot, here, :].astype(F32)
            power = f_re * f_re + f_im * f_im
            factor = amp * lax.rsqrt(jnp.maximum(power, FLOOR_SQUARED)) - 1.0
            tall[at, here, :] = (f_re * factor).astype(BF16)
            tall[at, frame + k : frame + k + step, :] = (f_im * factor).astype(BF16)

    def leave(slot, at):
        row, base, shift = place(slot)
        for k in chunks:
            rows = pl.ds(pl.multiple_of(row + k, step), step)
            here = pl.ds(k, step)
            x_re = field[at, here, :frame]
            x_im = field[at, here, frame:]
            p_re, p_im = probe_ref[0, here, :], probe_ref[1, here, :]
            for plane, value in enumerate((p_re * x_re + p_im * x_im, p_re * x_im - p_im * x_re)):
                turned = [
                    pltpu.roll(value[:, t * LANES : (t + 1) * LANES], shift, 1) for t in range(tiles)
                ]
                for tile in range(tiles + 1):
                    if tile == 0:
                        part = jnp.where(lane >= shift, turned[0], 0.0)
                    elif tile == tiles:
                        part = jnp.where(lane < shift, turned[-1], 0.0)
                    else:
                        part = jnp.where(lane < shift, turned[tile - 1], turned[tile])
                    acc[plane, rows, columns(base, tile)] += part

    def run(slots):
        for at, slot in enumerate(slots):
            enter(slot, at)
            transform(at, first_ref, second_ref)
        for at, slot in enumerate(slots):
            constrain(slot, at)
            transform(at, second_ref, first_ref)
        for at, slot in enumerate(slots):
            leave(slot, at)

    def choice(live):
        @pl.when(count_ref[0] == live)
        def _():
            run(range(live))
            for at in range(live, amp_ref.shape[0]):
                field[at] = jnp.zeros(field.shape[1:], F32)
                patch[at] = jnp.zeros(patch.shape[1:], BF16)

    for live in range(1, amp_ref.shape[0] + 1):
        choice(live)


def frames(row_offset, col_offset, counts, obj, probe, amplitudes, first, second, acc):
    frame = probe.shape[1]
    slots = amplitudes.shape[0]
    in_vmem = pl.BlockSpec(memory_space=VMEM)
    in_smem = pl.BlockSpec(memory_space=pltpu.SMEM)
    return pl.pallas_call(
        frames_kernel,
        out_shape=(
            jax.ShapeDtypeStruct(acc.shape, F32),
            jax.ShapeDtypeStruct((slots, frame, 2 * frame), F32),
            jax.ShapeDtypeStruct((slots, 2, frame, frame), BF16),
        ),
        in_specs=[in_smem] * 3 + [in_vmem] * 6,
        out_specs=(in_vmem, in_vmem, in_vmem),
        input_output_aliases={8: 0},
        scratch_shapes=[
            VMEM((slots, 2 * frame, frame), BF16),
            VMEM((slots, frame, 2 * frame), BF16),
        ],
        compiler_params=pltpu.CompilerParams(vmem_limit_bytes=14 << 20),
        name="frames",
    )(row_offset, col_offset, counts, obj, probe, amplitudes, first, second, acc)


def encode(value):
    rows = lax.broadcasted_iota(jnp.int32, value.shape, value.ndim - 2)
    peak = jnp.max(jnp.abs(value), axis=-2, keepdims=True)
    power = jnp.ceil(jnp.log2(jnp.maximum(peak, 1e-30)) + 0.01)
    bits = (power.astype(jnp.int32) + CODE_BIAS) >> (rows % 8)
    whole = jnp.round(value * jnp.exp2(CODE_BITS - power)).astype(jnp.int32)
    return (2 * whole + (bits & 1)).astype(jnp.int16)


def decode(code):
    code = code.astype(jnp.int32)
    rows = lax.broadcasted_iota(jnp.int32, code.shape, code.ndim - 2)
    low = code & 1
    bits = jnp.where(rows < 8, low << (rows % 8), 0)
    power = jnp.sum(bits, axis=-2, keepdims=True) - CODE_BIAS
    return (code - low).astype(F32) * jnp.exp2(power.astype(F32) - (CODE_BITS + 1))


def merge_kernel(
    rows_n, cols_n, with_probe, acc_ref, back_ref, patch_ref, probe_ref, field_ref, share_ref, out_ref,
    sum_ref, got_corner, got_low, got_edge, got_top, total, low_left,
    right_corner, left_corner, right_edge, left_edge, to_down, from_up,
    got_sum, give, gotten, mine_code, sib_code, sems, psems, asems, fsems,
    pair_in, all_in,
):
    r = lax.axis_index("row")
    c = lax.axis_index("col")
    m = lax.axis_index("mode")
    half, _, tile_c = share_ref.shape
    tile_r = 2 * half
    frame = probe_ref.shape[1]
    near = frame - SHIFT - half
    has_up, has_down = r > 0, r < rows_n - 1
    has_left, has_right = c > 0, c < cols_n - 1
    whole = m == 0
    sib = {"mode": 1 - m}
    up, down = {"row": r - 1}, {"row": r + 1}
    left, right = {"col": c - 1}, {"col": c + 1}
    always = m >= 0
    steps = [(a, b) for a in range(rows_n) for b in range(cols_n) if a or b]
    places = [(lax.rem(r + a, rows_n), lax.rem(c + b, cols_n)) for a, b in steps]
    peers = [{"row": a, "col": b} for a, b in places]
    if with_probe:
        others = [(always, p) for p in peers]
    else:
        others = [(has_up, up), (has_down, down), (has_left, left), (has_right, right)]
    barrier = pltpu.get_barrier_semaphore()

    @pl.when(m == 1)
    def _():
        pl.semaphore_signal(barrier, inc=1, device_id=sib, device_id_type=MESH)

    expected = 2 * greet([(present, {**where, "mode": 1}) for present, where in others])

    def block(which, base):
        return pl.ds(pl.multiple_of(which * half + base, half), half)

    top_mine, low_mine = block(m, 0), block(m, tile_r)
    top_sib, low_sib = block(1 - m, 0), block(1 - m, tile_r)
    body, edge = pl.ds(0, tile_c), pl.ds(tile_c, frame)
    first, rest = pl.ds(0, frame), pl.ds(frame, tile_c - frame)
    near_rows, far_rows = pl.ds(0, near), pl.ds(near, half - near)
    sum_rows = frame // 2
    shard = sum_rows // (rows_n * cols_n)

    def chip(row, col):
        return row * cols_n + col

    def rows_of(row, col, base=0):
        return pl.ds(pl.multiple_of(base + chip(row, col) * shard, shard), shard)

    def add_up(base):
        for k in range(0, sum_rows, STEP):
            here = pl.ds(pl.multiple_of(base + k, STEP), STEP)
            grad_re = grad_im = weight = 0.0
            for at in range(patch_ref.shape[0]):
                x_re = back_ref[at, here, :frame]
                x_im = back_ref[at, here, frame:]
                o_re = patch_ref[at, 0, here, :].astype(F32)
                o_im = patch_ref[at, 1, here, :].astype(F32)
                grad_re = grad_re + (o_re * x_re + o_im * x_im)
                grad_im = grad_im + (o_re * x_im - o_im * x_re)
                weight = weight + (o_re * o_re + o_im * o_im)
            sum_ref[0, here, :] = grad_re
            sum_ref[1, here, :] = grad_im
            sum_ref[2, here, :] = weight

    if with_probe:
        add_up((1 - m) * sum_rows)

    @pl.when(m == 0)
    def _():
        pl.semaphore_wait(barrier, 1)
        pl.semaphore_signal(pair_in, inc=1, device_id=sib, device_id_type=MESH)

    @pl.when(m == 1)
    def _():
        pl.semaphore_wait(pair_in, 1)

    if with_probe:
        away = pl.ds(pl.multiple_of((1 - m) * sum_rows, sum_rows), sum_rows)
        swap_sum = remote(sum_ref.at[:, away, :], got_sum, psems, 0, sib)
        swap_sum.start()
    swap_corner = remote(acc_ref.at[:, low_sib, edge], got_corner, sems, 0, sib)
    swap_low = remote(acc_ref.at[:, low_sib, body], got_low, sems, 1, sib)
    swap_edge = remote(acc_ref.at[:, top_sib, edge], got_edge, sems, 2, sib)
    swap_top = remote(acc_ref.at[:, top_sib, body], got_top, sems, 3, sib)

    @pl.when(has_right & has_down)
    def _():
        swap_corner.start()

    @pl.when(has_down)
    def _():
        swap_low.start()

    @pl.when(has_right)
    def _():
        swap_edge.start()

    swap_top.start()

    def part(src, dst, rows, cols, slot, where):
        return remote(src.at[:, rows, cols], dst.at[:, rows, cols], sems, slot, where)

    corner_near = part(right_corner, left_corner, near_rows, first, 4, right)
    corner_far = part(right_corner, left_corner, far_rows, first, 5, right)
    side = remote(right_edge, left_edge, sems, 6, right)
    rest_near = part(to_down, from_up, near_rows, rest, 7, down)
    rest_far = part(to_down, from_up, far_rows, rest, 8, down)
    first_near = part(to_down, from_up, near_rows, first, 9, down)
    first_far = part(to_down, from_up, far_rows, first, 10, down)

    def both(near_copy, far_copy, act):
        act(near_copy)

        @pl.when(whole)
        def _():
            act(far_copy)

    start, recv, sent = (lambda x: x.start()), (lambda x: x.wait_recv()), (lambda x: x.wait_send())

    if with_probe:
        own = chip(r, c)
        base = m * sum_rows
        add_up(base)
        swap_sum.wait_recv()
        for k, (row, col) in enumerate(places):
            value = sum_ref[:, rows_of(row, col, base), :] + got_sum[:, rows_of(row, col), :]
            give[k] = encode(value)

    @pl.when(m == 1)
    def _():
        pl.semaphore_wait(barrier, expected)
        pl.semaphore_signal(all_in, inc=1, device_id=sib, device_id_type=MESH)

    @pl.when(m == 0)
    def _():
        pl.semaphore_wait(all_in, 1)

    if with_probe:
        scatter = []
        for k in range(len(steps)):
            scatter.append(remote(give.at[k], gotten.at[k], psems, 1 + k, peers[k]))
            scatter[-1].start()

    @pl.when(has_right & has_down)
    def _():
        swap_corner.wait_recv()
        right_corner[...] = (acc_ref[:, low_mine, edge] + got_corner[...]).astype(BF16)
        both(corner_near, corner_far, start)

    @pl.when(has_down)
    def _():
        swap_low.wait_recv()
        to_down[:, :, rest] = (acc_ref[:, low_mine, rest] + got_low[:, :, rest]).astype(BF16)
        low_left[...] = acc_ref[:, low_mine, first] + got_low[:, :, first]

    @pl.when(has_right)
    def _():
        swap_edge.wait_recv()
        right_edge[...] = (acc_ref[:, top_mine, edge] + got_edge[...]).astype(BF16)

    swap_top.wait_recv()
    total[...] = acc_ref[:, top_mine, body] + got_top[...]
    peak = probe_ref[0] * probe_ref[0] + probe_ref[1] * probe_ref[1]
    peak = jnp.max(peak, keepdims=True) + EPSILON
    if with_probe:
        for copy in scatter:
            copy.wait_send()

    @pl.when(has_down)
    def _():
        both(rest_near, rest_far, start)

    @pl.when(has_right)
    def _():
        side.start()

    @pl.when(has_left & has_down)
    def _():
        corner_near.wait_recv()
        low_left[:, near_rows, :] += left_corner[:, near_rows, :].astype(F32)

        @pl.when(whole)
        def _():
            corner_far.wait_recv()
            low_left[:, far_rows, :] += left_corner[:, far_rows, :].astype(F32)

    @pl.when(has_down)
    def _():
        to_down[:, :, first] = low_left[...].astype(BF16)
        both(first_near, first_far, start)

    if with_probe:
        value = sum_ref[:, rows_of(r, c, base), :] + got_sum[:, rows_of(r, c), :]
        for k in range(len(steps)):
            scatter[k].wait_recv()
            value = value + decode(gotten[k])
        weight = value[2:] + REGULARIZER
        mine_code[own] = encode(value[:2] / weight)
        spread, crossings = [], []
        for k in range(len(steps)):
            spread.append(remote(mine_code.at[own], mine_code.at[own], asems, k, peers[k]))
            spread[-1].start()
        crossings.append(remote(mine_code.at[own], sib_code.at[own], fsems, 0, sib))
        crossings[0].start()
    else:
        out_ref[...] = jnp.zeros_like(out_ref)

    @pl.when(has_left)
    def _():
        side.wait_recv()
        total[:, :, first] += left_edge[...].astype(F32)

    @pl.when(has_up)
    def _():
        rest_near.wait_recv()
        first_near.wait_recv()
        total[:, near_rows, :] += from_up[:, near_rows, :].astype(F32)

        @pl.when(whole)
        def _():
            rest_far.wait_recv()
            first_far.wait_recv()
            total[:, far_rows, :] += from_up[:, far_rows, :].astype(F32)

    for plane in range(2):
        share_ref[:, plane, :] = field_ref[top_mine, plane, :] + total[plane] / peak

    if with_probe:

        def finish(codes, row, col, base):
            rows = rows_of(row, col, base)
            fresh = probe_ref[:, rows, :] + decode(codes[chip(row, col)])
            for plane in range(2):
                out_ref[rows, plane, :] = fresh[plane]

        origins = [(lax.rem(r + rows_n - a, rows_n), lax.rem(c + cols_n - b, cols_n)) for a, b in steps]
        for k, (row, col) in enumerate(origins):
            spread[k].wait_recv()
            at = chip(row, col)
            crossings.append(remote(mine_code.at[at], sib_code.at[at], fsems, 1 + k, sib))
            crossings[-1].start()
        for row, col in [(r, c)] + origins:
            finish(mine_code, row, col, base)
        for k, (row, col) in enumerate([(r, c)] + origins):
            crossings[k].wait_recv()
            finish(sib_code, row, col, sum_rows - base)

    swap_top.wait_send()

    @pl.when(has_right)
    def _():
        swap_edge.wait_send()
        side.wait_send()

    @pl.when(has_down)
    def _():
        swap_low.wait_send()
        both(rest_near, rest_far, sent)
        both(first_near, first_far, sent)

    @pl.when(has_right & has_down)
    def _():
        swap_corner.wait_send()
        both(corner_near, corner_far, sent)

    if with_probe:
        swap_sum.wait_send()
        for copy in spread + crossings:
            copy.wait_send()


def merge(acc, back, patch, probe, field, rows_n, cols_n, with_probe):
    tile_r, _, tile_c = field.shape
    frame = probe.shape[1]
    half = tile_r // 2
    sum_rows = frame // 2
    chips = rows_n * cols_n if with_probe else 2
    shard = sum_rows // chips if with_probe else 16
    in_vmem = pl.BlockSpec(memory_space=VMEM)
    return pl.pallas_call(
        functools.partial(merge_kernel, rows_n, cols_n, with_probe),
        out_shape=(
            jax.ShapeDtypeStruct((half, 2, tile_c), F32),
            jax.ShapeDtypeStruct((frame, 2, frame), F32),
        ),
        in_specs=[in_vmem] * 5,
        out_specs=(in_vmem, in_vmem),
        scratch_shapes=[
            VMEM((3, frame, frame), F32),
            VMEM((2, half, frame), F32),
            VMEM((2, half, tile_c), F32),
            VMEM((2, half, frame), F32),
            VMEM((2, half, tile_c), F32),
            VMEM((2, half, tile_c), F32),
            VMEM((2, half, frame), F32),
            VMEM((2, half, frame), BF16),
            VMEM((2, half, frame), BF16),
            VMEM((2, half, frame), BF16),
            VMEM((2, half, frame), BF16),
            VMEM((2, half, tile_c), BF16),
            VMEM((2, half, tile_c), BF16),
            VMEM((3, sum_rows, frame), F32),
            VMEM((chips - 1, 3, shard, frame), jnp.int16),
            VMEM((chips - 1, 3, shard, frame), jnp.int16),
            VMEM((chips, 2, shard, frame), jnp.int16),
            VMEM((chips, 2, shard, frame), jnp.int16),
            pltpu.SemaphoreType.DMA((2, 11)),
            pltpu.SemaphoreType.DMA((2, chips)),
            pltpu.SemaphoreType.DMA((2, chips)),
            pltpu.SemaphoreType.DMA((2, chips)),
            pltpu.SemaphoreType.REGULAR,
            pltpu.SemaphoreType.REGULAR,
        ],
        compiler_params=pltpu.CompilerParams(
            collective_id=1, has_side_effects=True, vmem_limit_bytes=16 << 20
        ),
        name="merge",
    )(acc, back, patch, probe, field)


def store_kernel(share_ref, fresh_ref, share_hbm, fresh_hbm, sems):
    pairs = [(share_ref, share_hbm), (fresh_ref, fresh_hbm)]
    copies = [pltpu.make_async_copy(a, b, sems.at[i]) for i, (a, b) in enumerate(pairs)]
    for copy in copies:
        copy.start()
    for copy in copies:
        copy.wait()


def store(share, fresh):
    return pl.pallas_call(
        store_kernel,
        out_shape=tuple(jax.ShapeDtypeStruct(x.shape, x.dtype) for x in (share, fresh)),
        in_specs=[pl.BlockSpec(memory_space=VMEM)] * 2,
        out_specs=(pl.BlockSpec(memory_space=pltpu.HBM),) * 2,
        scratch_shapes=[pltpu.SemaphoreType.DMA((2,))],
        compiler_params=pltpu.CompilerParams(vmem_limit_bytes=1 << 20),
        name="store",
    )(share, fresh)


def body(rows_n, cols_n, object_field, probe_field, amplitudes, row_offset, col_offset, counts):
    frame = probe_field.shape[0]
    first, second = dft_tables(frame)
    extras = (row_offset, col_offset, amplitudes, first, second)
    obj, probe, acc, *extras = halo(object_field, probe_field, extras, rows_n, cols_n)
    rows, cols, amplitudes, first, second = extras
    acc, back, patch = frames(rows, cols, counts, obj, probe, amplitudes, first, second, acc)
    with_probe = frame % (2 * rows_n * cols_n * 16) == 0
    object_new, fresh = merge(
        acc, back, patch, probe, object_field, rows_n, cols_n, with_probe
    )
    if not with_probe:
        x_re, x_im = back[:, :, :frame], back[:, :, frame:]
        o_re, o_im = patch[:, 0].astype(F32), patch[:, 1].astype(F32)
        grad = [o_re * x_re + o_im * x_im, o_re * x_im - o_im * x_re]
        sums = jnp.stack([x.sum(0) for x in (*grad, o_re * o_re + o_im * o_im)])
        sums = lax.psum(sums, ("row", "col", "mode"))
        fresh = probe + sums[:2] / (sums[2:] + REGULARIZER)
        fresh = jnp.moveaxis(fresh, 0, 1)
    return store(object_new, fresh)


def solution(mesh):
    split = ("groups", "row", "col", "mode")
    placed = (
        P(("groups", "row"), None, "col"),
        P("groups", None, None),
        P(split, None, None),
        P(split),
        P(split),
        P(split),
    )
    return jax.shard_map(
        functools.partial(body, mesh.shape["row"], mesh.shape["col"]),
        mesh=mesh,
        in_specs=placed,
        out_specs=(P(("groups", "row", "mode"), None, "col"), P("groups", None, None)),
        check_vma=False,
    )
```

```python
import functools
import math

import jax
import jax.numpy as jnp
import numpy as np
from jax import lax
from jax.experimental import pallas as pl
from jax.experimental.pallas import tpu as pltpu
from jax.sharding import PartitionSpec as P

FLOOR_SQUARED = 0.25
EPSILON = 1e-05
REGULARIZER = 1.0
F32 = jnp.float32
BF16 = jnp.bfloat16
MESH = pl.DeviceIdType.MESH
VMEM = pltpu.VMEM
LANES = 128
SHIFT = 64
CODE_BITS = 14
CODE_BIAS = 120
PIECE = 32
AHEAD = 2
STEP = 16


def dft_tables(points):
    index = np.arange(points)
    product = (index[:, None] * index[None, :]) % points
    angle = (2.0 * math.pi / points) * product.astype(np.float32)
    norm = np.float32(1.0 / math.sqrt(points))
    cosine = (np.cos(angle.astype(np.float32)) * norm).astype(np.float32)
    sine = (np.sin(angle.astype(np.float32)) * norm).astype(np.float32)
    first = np.block([[cosine, sine], [-sine, cosine]])
    second = np.block([[cosine, -sine], [sine, cosine]])
    return jnp.asarray(first, BF16), jnp.asarray(second, BF16)


def greet(peers):
    barrier = pltpu.get_barrier_semaphore()
    expected = jnp.int32(0)
    for present, where in peers:
        expected = expected + present.astype(jnp.int32)

        @pl.when(present)
        def _(where=where):
            pl.semaphore_signal(barrier, inc=1, device_id=where, device_id_type=MESH)

    return expected


def remote(src, dst, sems, slot, where):
    return pltpu.make_async_remote_copy(
        src_ref=src,
        dst_ref=dst,
        send_sem=sems.at[0, slot],
        recv_sem=sems.at[1, slot],
        device_id=where,
        device_id_type=MESH,
    )


def halo_kernel(rows_n, cols_n, count, *refs):
    field_hbm, probe_hbm = refs[:2]
    extras = refs[2 : 2 + count]
    obj_ref, planes_ref, acc_ref = refs[2 + count : 5 + count]
    landed = refs[5 + count : 5 + 2 * count]
    field_ref, probe_ref, sems, local = refs[5 + 2 * count :]
    r = lax.axis_index("row")
    c = lax.axis_index("col")
    m = lax.axis_index("mode")
    tile_r, _, tile_c = field_ref.shape
    frame = probe_ref.shape[0]
    half, reach = tile_r // 2, frame - SHIFT
    low = reach // 2
    chunks = tile_r // PIECE
    strips = [
        pl.ds(pl.multiple_of(lax.rem(m * (low // PIECE) + k, chunks) * PIECE, PIECE), PIECE)
        for k in range(chunks)
    ]
    pairs = [(field_hbm.at[strip], field_ref.at[strip]) for strip in strips]
    pairs += [(probe_hbm, probe_ref), *zip(extras, landed)]
    fetches = [pltpu.make_async_copy(a, b, local.at[i]) for i, (a, b) in enumerate(pairs)]
    for fetch in fetches[:chunks]:
        fetch.start()
    has_up, has_down = r > 0, r < rows_n - 1
    has_left, has_right = c > 0, c < cols_n - 1
    sib = {"mode": 1 - m}
    up, down = {"row": r - 1}, {"row": r + 1}
    left, right = {"col": c - 1}, {"col": c + 1}
    always = m >= 0
    below_right = {"row": r + 1, "col": c + 1}
    greet([(always, sib), (has_down, down), (has_right, right), (has_down & has_right, below_right)])
    ups, lefts = has_up.astype(jnp.int32), has_left.astype(jnp.int32)
    expected = 1 + ups + lefts + ups * lefts
    mine = pl.ds(pl.multiple_of(m * half, half), half)
    lift = pl.ds(pl.multiple_of(m * low, 32), low)
    below = pl.ds(pl.multiple_of(tile_r + m * low, 32), low)
    first, rest, edge = pl.ds(0, frame), pl.ds(frame, tile_c - frame), pl.ds(tile_c, frame)

    def part(rows, cols, to_rows, to_cols, slot, where):
        return remote(
            obj_ref.at[:, rows, cols], obj_ref.at[:, to_rows, to_cols], sems, slot, where
        )

    pieces = [pl.ds(pl.multiple_of(m * low + k, PIECE), PIECE) for k in range(0, low, PIECE)]
    landing = [
        pl.ds(pl.multiple_of(tile_r + m * low + k, PIECE), PIECE) for k in range(0, low, PIECE)
    ]
    n = len(pieces)
    up_first = [part(a, first, b, first, k, up) for k, (a, b) in enumerate(zip(pieces, landing))]
    corner = [part(b, first, b, edge, n + k, left) for k, b in enumerate(landing[:-1])]
    across = {"row": r - 1, "col": c - 1}
    corner.append(part(pieces[-1], first, landing[-1], edge, 2 * n - 1, across))
    swap_corner = [part(b, edge, b, edge, 2 * n + k, sib) for k, b in enumerate(landing)]
    to_left = part(mine, first, mine, edge, 3 * n, left)
    up_rest = part(lift, rest, below, rest, 3 * n + 1, up)
    swap_edge = part(mine, edge, mine, edge, 3 * n + 2, sib)
    swap_first = part(below, first, below, first, 3 * n + 3, sib)
    swap_rest = part(below, rest, below, rest, 3 * n + 4, sib)

    def convert(k):
        fetches[k].wait()
        for plane in range(2):
            obj_ref[plane, strips[k], :tile_c] = field_ref[strips[k], plane, :].astype(BF16)

    for k in range(n):
        convert(k)
        if k == 0:
            pl.semaphore_wait(pltpu.get_barrier_semaphore(), expected)

        @pl.when(has_up)
        def _(k=k):
            up_first[k].start()

    @pl.when(has_up & has_left)
    def _():
        corner[-1].start()

    for fetch in fetches[chunks:]:
        fetch.start()
    enough = (tile_r - low) // PIECE
    for k in range(n, enough):
        convert(k)

    @pl.when(has_left)
    def _():
        to_left.start()

    for k in range(enough, chunks):
        convert(k)
    fetches[chunks].wait()
    for plane in range(2):
        planes_ref[plane] = probe_ref[:, plane, :]
    acc_ref[...] = jnp.zeros(acc_ref.shape, F32)

    @pl.when(has_up)
    def _():
        for copy in up_first[:AHEAD]:
            copy.wait_send()
        up_rest.start()

    @pl.when(has_down)
    def _():
        for k in range(n):
            up_first[k].wait_recv()
            if k < n - 1:

                @pl.when(has_left)
                def _(k=k):
                    corner[k].start()

        swap_first.start()

    @pl.when(has_right)
    def _():
        to_left.wait_recv()
        swap_edge.start()

    def turn(k):
        @pl.when(has_right & has_down)
        def _():
            corner[k].wait_recv()
            swap_corner[k].start()

    turn(0)

    @pl.when(has_down)
    def _():
        up_rest.wait_recv()
        swap_rest.start()

    for k in range(1, n):
        turn(k)

    @pl.when(has_right)
    def _():
        swap_edge.wait()

    @pl.when(has_down)
    def _():
        swap_first.wait()
        swap_rest.wait()

        @pl.when(has_left)
        def _():
            for copy in corner[:-1]:
                copy.wait_send()

    @pl.when(has_up & has_left)
    def _():
        corner[-1].wait_send()

    @pl.when(has_left)
    def _():
        to_left.wait_send()

    @pl.when(has_up)
    def _():
        for copy in up_first[AHEAD:]:
            copy.wait_send()
        up_rest.wait_send()

    @pl.when(has_right & has_down)
    def _():
        for copy in swap_corner:
            copy.wait()

    for fetch in fetches[chunks + 1 :]:
        fetch.wait()


def halo(field, probe, extras, rows_n, cols_n):
    tile_r, planes, tile_c = field.shape
    frame = probe.shape[0]
    shape = (planes, tile_r + frame, tile_c + frame)
    in_vmem = pl.BlockSpec(memory_space=VMEM)
    return pl.pallas_call(
        functools.partial(halo_kernel, rows_n, cols_n, len(extras)),
        out_shape=(
            jax.ShapeDtypeStruct(shape, BF16),
            jax.ShapeDtypeStruct((planes, frame, frame), F32),
            jax.ShapeDtypeStruct(shape, F32),
            *(jax.ShapeDtypeStruct(x.shape, x.dtype) for x in extras),
        ),
        in_specs=[pl.BlockSpec(memory_space=pltpu.HBM)] * (2 + len(extras)),
        out_specs=(in_vmem,) * (3 + len(extras)),
        scratch_shapes=[
            VMEM(field.shape, F32),
            VMEM(probe.shape, F32),
            pltpu.SemaphoreType.DMA((2, 5 + 3 * ((frame - SHIFT) // 2 // PIECE))),
            pltpu.SemaphoreType.DMA((tile_r // PIECE + 1 + len(extras),)),
        ],
        cost_estimate=pl.CostEstimate(flops=0, bytes_accessed=40 << 20, transcendentals=0),
        compiler_params=pltpu.CompilerParams(
            collective_id=0, has_side_effects=True, vmem_limit_bytes=8 << 20
        ),
        name="halo",
    )(*(pltpu.with_memory_space_constraint(x, pltpu.HBM) for x in (field, probe, *extras)))


def frames_kernel(
    row_ref, col_ref, count_ref, obj, probe_ref, amp_ref, first_ref, second_ref, _zero,
    acc, field, patch, tall, wide,
):
    frame = probe_ref.shape[1]
    ext_rows, ext_cols = obj.shape[1:]
    top = lax.axis_index("row") * (ext_rows - frame)
    left = lax.axis_index("col") * (ext_cols - frame)
    step = 32
    chunks = range(0, frame, step)
    tiles = frame // LANES
    lane = lax.broadcasted_iota(jnp.int32, (step, LANES), 1)

    def place(slot):
        row = row_ref[slot] - top
        col = col_ref[slot] - left
        return row, (col // LANES) * LANES, col % LANES

    def columns(base, tile):
        return pl.ds(pl.multiple_of(base + tile * LANES, LANES), LANES)

    def enter(slot, at):
        row, base, shift = place(slot)
        for k in chunks:
            rows = pl.ds(pl.multiple_of(row + k, step), step)
            here = pl.ds(k, step)
            for plane in range(2):
                turned = []
                for tile in range(tiles + 1):
                    value = obj[plane, rows, columns(base, tile)].astype(F32)
                    turned.append(pltpu.roll(value, shift, 1))
                for tile in range(tiles):
                    value = jnp.where(lane < LANES - shift, turned[tile], turned[tile + 1])
                    patch[at, plane, here, tile * LANES : (tile + 1) * LANES] = value.astype(BF16)
            o_re, o_im = patch[at, 0, here, :].astype(F32), patch[at, 1, here, :].astype(F32)
            p_re, p_im = probe_ref[0, here, :], probe_ref[1, here, :]
            tall[at, here, :] = (p_re * o_re - p_im * o_im).astype(BF16)
            tall[at, frame + k : frame + k + step, :] = (p_re * o_im + p_im * o_re).astype(BF16)

    def transform(at, one_ref, two_ref):
        half = jnp.dot(one_ref[...], tall[at], preferred_element_type=F32).astype(BF16)
        wide[at, :, :frame] = half[:frame]
        wide[at, :, frame:] = half[frame:]
        field[at] = jnp.dot(wide[at], two_ref[...], preferred_element_type=F32)

    def constrain(slot, at):
        for k in chunks:
            here = pl.ds(k, step)
            f_re = field[at, here, :frame]
            f_im = field[at, here, frame:]
            amp = amp_ref[slot, here, :].astype(F32)
            power = f_re * f_re + f_im * f_im
            factor = amp * lax.rsqrt(jnp.maximum(power, FLOOR_SQUARED)) - 1.0
            tall[at, here, :] = (f_re * factor).astype(BF16)
            tall[at, frame + k : frame + k + step, :] = (f_im * factor).astype(BF16)

    def leave(slot, at):
        row, base, shift = place(slot)
        for k in chunks:
            rows = pl.ds(pl.multiple_of(row + k, step), step)
            here = pl.ds(k, step)
            x_re = field[at, here, :frame]
            x_im = field[at, here, frame:]
            p_re, p_im = probe_ref[0, here, :], probe_ref[1, here, :]
            for plane, value in enumerate((p_re * x_re + p_im * x_im, p_re * x_im - p_im * x_re)):
                turned = [
                    pltpu.roll(value[:, t * LANES : (t + 1) * LANES], shift, 1) for t in range(tiles)
                ]
                for tile in range(tiles + 1):
                    if tile == 0:
                        part = jnp.where(lane >= shift, turned[0], 0.0)
                    elif tile == tiles:
                        part = jnp.where(lane < shift, turned[-1], 0.0)
                    else:
                        part = jnp.where(lane < shift, turned[tile - 1], turned[tile])
                    acc[plane, rows, columns(base, tile)] += part

    def run(slots):
        for at, slot in enumerate(slots):
            enter(slot, at)
            transform(at, first_ref, second_ref)
        for at, slot in enumerate(slots):
            constrain(slot, at)
            transform(at, second_ref, first_ref)
        for at, slot in enumerate(slots):
            leave(slot, at)

    def choice(live):
        @pl.when(count_ref[0] == live)
        def _():
            run(range(live))
            for at in range(live, amp_ref.shape[0]):
                field[at] = jnp.zeros(field.shape[1:], F32)
                patch[at] = jnp.zeros(patch.shape[1:], BF16)

    for live in range(1, amp_ref.shape[0] + 1):
        choice(live)


def frames(row_offset, col_offset, counts, obj, probe, amplitudes, first, second, acc):
    frame = probe.shape[1]
    slots = amplitudes.shape[0]
    in_vmem = pl.BlockSpec(memory_space=VMEM)
    in_smem = pl.BlockSpec(memory_space=pltpu.SMEM)
    return pl.pallas_call(
        frames_kernel,
        out_shape=(
            jax.ShapeDtypeStruct(acc.shape, F32),
            jax.ShapeDtypeStruct((slots, frame, 2 * frame), F32),
            jax.ShapeDtypeStruct((slots, 2, frame, frame), BF16),
        ),
        in_specs=[in_smem] * 3 + [in_vmem] * 6,
        out_specs=(in_vmem, in_vmem, in_vmem),
        input_output_aliases={8: 0},
        scratch_shapes=[
            VMEM((slots, 2 * frame, frame), BF16),
            VMEM((slots, frame, 2 * frame), BF16),
        ],
        compiler_params=pltpu.CompilerParams(vmem_limit_bytes=14 << 20),
        name="frames",
    )(row_offset, col_offset, counts, obj, probe, amplitudes, first, second, acc)


def encode(value):
    rows = lax.broadcasted_iota(jnp.int32, value.shape, value.ndim - 2)
    peak = jnp.max(jnp.abs(value), axis=-2, keepdims=True)
    power = jnp.ceil(jnp.log2(jnp.maximum(peak, 1e-30)) + 0.01)
    bits = (power.astype(jnp.int32) + CODE_BIAS) >> (rows % 8)
    whole = jnp.round(value * jnp.exp2(CODE_BITS - power)).astype(jnp.int32)
    return (2 * whole + (bits & 1)).astype(jnp.int16)


def decode(code):
    code = code.astype(jnp.int32)
    rows = lax.broadcasted_iota(jnp.int32, code.shape, code.ndim - 2)
    low = code & 1
    bits = jnp.where(rows < 8, low << (rows % 8), 0)
    power = jnp.sum(bits, axis=-2, keepdims=True) - CODE_BIAS
    return (code - low).astype(F32) * jnp.exp2(power.astype(F32) - (CODE_BITS + 1))


def merge_kernel(
    rows_n, cols_n, with_probe, acc_ref, back_ref, patch_ref, probe_ref, field_ref, share_ref, out_ref,
    sum_ref, got_corner, got_low, got_edge, got_top, total, low_left,
    right_corner, left_corner, right_edge, left_edge, to_down, from_up,
    got_sum, give, gotten, mine_code, sib_code, sems, psems, asems, fsems,
    pair_in, all_in,
):
    r = lax.axis_index("row")
    c = lax.axis_index("col")
    m = lax.axis_index("mode")
    half, _, tile_c = share_ref.shape
    tile_r = 2 * half
    frame = probe_ref.shape[1]
    near = frame - SHIFT - half
    has_up, has_down = r > 0, r < rows_n - 1
    has_left, has_right = c > 0, c < cols_n - 1
    whole = m == 0
    sib = {"mode": 1 - m}
    up, down = {"row": r - 1}, {"row": r + 1}
    left, right = {"col": c - 1}, {"col": c + 1}
    always = m >= 0
    steps = [(a, b) for a in range(rows_n) for b in range(cols_n) if a or b]
    places = [(lax.rem(r + a, rows_n), lax.rem(c + b, cols_n)) for a, b in steps]
    peers = [{"row": a, "col": b} for a, b in places]
    if with_probe:
        others = [(always, p) for p in peers]
    else:
        others = [(has_up, up), (has_down, down), (has_left, left), (has_right, right)]
    barrier = pltpu.get_barrier_semaphore()

    @pl.when(m == 1)
    def _():
        pl.semaphore_signal(barrier, inc=1, device_id=sib, device_id_type=MESH)

    expected = 2 * greet([(present, {**where, "mode": 1}) for present, where in others])

    def block(which, base):
        return pl.ds(pl.multiple_of(which * half + base, half), half)

    top_mine, low_mine = block(m, 0), block(m, tile_r)
    top_sib, low_sib = block(1 - m, 0), block(1 - m, tile_r)
    body, edge = pl.ds(0, tile_c), pl.ds(tile_c, frame)
    first, rest = pl.ds(0, frame), pl.ds(frame, tile_c - frame)
    near_rows, far_rows = pl.ds(0, near), pl.ds(near, half - near)
    sum_rows = frame // 2
    shard = sum_rows // (rows_n * cols_n)

    def chip(row, col):
        return row * cols_n + col

    def rows_of(row, col, base=0):
        return pl.ds(pl.multiple_of(base + chip(row, col) * shard, shard), shard)

    def add_up(base):
        for k in range(0, sum_rows, STEP):
            here = pl.ds(pl.multiple_of(base + k, STEP), STEP)
            grad_re = grad_im = weight = 0.0
            for at in range(patch_ref.shape[0]):
                x_re = back_ref[at, here, :frame]
                x_im = back_ref[at, here, frame:]
                o_re = patch_ref[at, 0, here, :].astype(F32)
                o_im = patch_ref[at, 1, here, :].astype(F32)
                grad_re = grad_re + (o_re * x_re + o_im * x_im)
                grad_im = grad_im + (o_re * x_im - o_im * x_re)
                weight = weight + (o_re * o_re + o_im * o_im)
            sum_ref[0, here, :] = grad_re
            sum_ref[1, here, :] = grad_im
            sum_ref[2, here, :] = weight

    if with_probe:
        add_up((1 - m) * sum_rows)

    @pl.when(m == 0)
    def _():
        pl.semaphore_wait(barrier, 1)
        pl.semaphore_signal(pair_in, inc=1, device_id=sib, device_id_type=MESH)

    @pl.when(m == 1)
    def _():
        pl.semaphore_wait(pair_in, 1)

    if with_probe:
        away = pl.ds(pl.multiple_of((1 - m) * sum_rows, sum_rows), sum_rows)
        swap_sum = remote(sum_ref.at[:, away, :], got_sum, psems, 0, sib)
        swap_sum.start()
    swap_corner = remote(acc_ref.at[:, low_sib, edge], got_corner, sems, 0, sib)
    swap_low = remote(acc_ref.at[:, low_sib, body], got_low, sems, 1, sib)
    swap_edge = remote(acc_ref.at[:, top_sib, edge], got_edge, sems, 2, sib)
    swap_top = remote(acc_ref.at[:, top_sib, body], got_top, sems, 3, sib)

    @pl.when(has_right & has_down)
    def _():
        swap_corner.start()

    @pl.when(has_down)
    def _():
        swap_low.start()

    @pl.when(has_right)
    def _():
        swap_edge.start()

    swap_top.start()

    def part(src, dst, rows, cols, slot, where):
        return remote(src.at[:, rows, cols], dst.at[:, rows, cols], sems, slot, where)

    corner_near = part(right_corner, left_corner, near_rows, first, 4, right)
    corner_far = part(right_corner, left_corner, far_rows, first, 5, right)
    side = remote(right_edge, left_edge, sems, 6, right)
    rest_near = part(to_down, from_up, near_rows, rest, 7, down)
    rest_far = part(to_down, from_up, far_rows, rest, 8, down)
    first_near = part(to_down, from_up, near_rows, first, 9, down)
    first_far = part(to_down, from_up, far_rows, first, 10, down)

    def both(near_copy, far_copy, act):
        act(near_copy)

        @pl.when(whole)
        def _():
            act(far_copy)

    start, recv, sent = (lambda x: x.start()), (lambda x: x.wait_recv()), (lambda x: x.wait_send())

    if with_probe:
        own = chip(r, c)
        base = m * sum_rows
        add_up(base)
        swap_sum.wait_recv()
        for k, (row, col) in enumerate(places):
            value = sum_ref[:, rows_of(row, col, base), :] + got_sum[:, rows_of(row, col), :]
            give[k] = encode(value)

    @pl.when(m == 1)
    def _():
        pl.semaphore_wait(barrier, expected)
        pl.semaphore_signal(all_in, inc=1, device_id=sib, device_id_type=MESH)

    @pl.when(m == 0)
    def _():
        pl.semaphore_wait(all_in, 1)

    if with_probe:
        scatter = []
        for k in range(len(steps)):
            scatter.append(remote(give.at[k], gotten.at[k], psems, 1 + k, peers[k]))
            scatter[-1].start()

    @pl.when(has_right & has_down)
    def _():
        swap_corner.wait_recv()
        right_corner[...] = (acc_ref[:, low_mine, edge] + got_corner[...]).astype(BF16)
        both(corner_near, corner_far, start)

    @pl.when(has_down)
    def _():
        swap_low.wait_recv()
        to_down[:, :, rest] = (acc_ref[:, low_mine, rest] + got_low[:, :, rest]).astype(BF16)
        low_left[...] = acc_ref[:, low_mine, first] + got_low[:, :, first]

    @pl.when(has_right)
    def _():
        swap_edge.wait_recv()
        right_edge[...] = (acc_ref[:, top_mine, edge] + got_edge[...]).astype(BF16)

    swap_top.wait_recv()
    total[...] = acc_ref[:, top_mine, body] + got_top[...]
    peak = probe_ref[0] * probe_ref[0] + probe_ref[1] * probe_ref[1]
    peak = jnp.max(peak, keepdims=True) + EPSILON
    if with_probe:
        for copy in scatter:
            copy.wait_send()

    @pl.when(has_down)
    def _():
        both(rest_near, rest_far, start)

    @pl.when(has_right)
    def _():
        side.start()

    @pl.when(has_left & has_down)
    def _():
        corner_near.wait_recv()
        low_left[:, near_rows, :] += left_corner[:, near_rows, :].astype(F32)

        @pl.when(whole)
        def _():
            corner_far.wait_recv()
            low_left[:, far_rows, :] += left_corner[:, far_rows, :].astype(F32)

    @pl.when(has_down)
    def _():
        to_down[:, :, first] = low_left[...].astype(BF16)
        both(first_near, first_far, start)

    if with_probe:
        value = sum_ref[:, rows_of(r, c, base), :] + got_sum[:, rows_of(r, c), :]
        for k in range(len(steps)):
            scatter[k].wait_recv()
            value = value + decode(gotten[k])
        weight = value[2:] + REGULARIZER
        mine_code[own] = encode(value[:2] / weight)
        spread, crossings = [], []
        for k in range(len(steps)):
            spread.append(remote(mine_code.at[own], mine_code.at[own], asems, k, peers[k]))
            spread[-1].start()
        crossings.append(remote(mine_code.at[own], sib_code.at[own], fsems, 0, sib))
        crossings[0].start()
    else:
        out_ref[...] = jnp.zeros_like(out_ref)

    @pl.when(has_left)
    def _():
        side.wait_recv()
        total[:, :, first] += left_edge[...].astype(F32)

    @pl.when(has_up)
    def _():
        rest_near.wait_recv()
        first_near.wait_recv()
        total[:, near_rows, :] += from_up[:, near_rows, :].astype(F32)

        @pl.when(whole)
        def _():
            rest_far.wait_recv()
            first_far.wait_recv()
            total[:, far_rows, :] += from_up[:, far_rows, :].astype(F32)

    for plane in range(2):
        share_ref[:, plane, :] = field_ref[top_mine, plane, :] + total[plane] / peak

    if with_probe:

        def finish(codes, row, col, base):
            rows = rows_of(row, col, base)
            fresh = probe_ref[:, rows, :] + decode(codes[chip(row, col)])
            for plane in range(2):
                out_ref[rows, plane, :] = fresh[plane]

        origins = [(lax.rem(r + rows_n - a, rows_n), lax.rem(c + cols_n - b, cols_n)) for a, b in steps]
        for k, (row, col) in enumerate(origins):
            spread[k].wait_recv()
            at = chip(row, col)
            crossings.append(remote(mine_code.at[at], sib_code.at[at], fsems, 1 + k, sib))
            crossings[-1].start()
        for row, col in [(r, c)] + origins:
            finish(mine_code, row, col, base)
        for k, (row, col) in enumerate([(r, c)] + origins):
            crossings[k].wait_recv()
            finish(sib_code, row, col, sum_rows - base)

    swap_top.wait_send()

    @pl.when(has_right)
    def _():
        swap_edge.wait_send()
        side.wait_send()

    @pl.when(has_down)
    def _():
        swap_low.wait_send()
        both(rest_near, rest_far, sent)
        both(first_near, first_far, sent)

    @pl.when(has_right & has_down)
    def _():
        swap_corner.wait_send()
        both(corner_near, corner_far, sent)

    if with_probe:
        swap_sum.wait_send()
        for copy in spread + crossings:
            copy.wait_send()


def merge(acc, back, patch, probe, field, rows_n, cols_n, with_probe):
    tile_r, _, tile_c = field.shape
    frame = probe.shape[1]
    half = tile_r // 2
    sum_rows = frame // 2
    chips = rows_n * cols_n if with_probe else 2
    shard = sum_rows // chips if with_probe else 16
    in_vmem = pl.BlockSpec(memory_space=VMEM)
    return pl.pallas_call(
        functools.partial(merge_kernel, rows_n, cols_n, with_probe),
        out_shape=(
            jax.ShapeDtypeStruct((half, 2, tile_c), F32),
            jax.ShapeDtypeStruct((frame, 2, frame), F32),
        ),
        in_specs=[in_vmem] * 5,
        out_specs=(in_vmem, in_vmem),
        scratch_shapes=[
            VMEM((3, frame, frame), F32),
            VMEM((2, half, frame), F32),
            VMEM((2, half, tile_c), F32),
            VMEM((2, half, frame), F32),
            VMEM((2, half, tile_c), F32),
            VMEM((2, half, tile_c), F32),
            VMEM((2, half, frame), F32),
            VMEM((2, half, frame), BF16),
            VMEM((2, half, frame), BF16),
            VMEM((2, half, frame), BF16),
            VMEM((2, half, frame), BF16),
            VMEM((2, half, tile_c), BF16),
            VMEM((2, half, tile_c), BF16),
            VMEM((3, sum_rows, frame), F32),
            VMEM((chips - 1, 3, shard, frame), jnp.int16),
            VMEM((chips - 1, 3, shard, frame), jnp.int16),
            VMEM((chips, 2, shard, frame), jnp.int16),
            VMEM((chips, 2, shard, frame), jnp.int16),
            pltpu.SemaphoreType.DMA((2, 11)),
            pltpu.SemaphoreType.DMA((2, chips)),
            pltpu.SemaphoreType.DMA((2, chips)),
            pltpu.SemaphoreType.DMA((2, chips)),
            pltpu.SemaphoreType.REGULAR,
            pltpu.SemaphoreType.REGULAR,
        ],
        compiler_params=pltpu.CompilerParams(
            collective_id=1, has_side_effects=True, vmem_limit_bytes=16 << 20
        ),
        name="merge",
    )(acc, back, patch, probe, field)


def store_kernel(share_ref, fresh_ref, share_hbm, fresh_hbm, sems):
    pairs = [(share_ref, share_hbm), (fresh_ref, fresh_hbm)]
    copies = [pltpu.make_async_copy(a, b, sems.at[i]) for i, (a, b) in enumerate(pairs)]
    for copy in copies:
        copy.start()
    for copy in copies:
        copy.wait()


def store(share, fresh):
    return pl.pallas_call(
        store_kernel,
        out_shape=tuple(jax.ShapeDtypeStruct(x.shape, x.dtype) for x in (share, fresh)),
        in_specs=[pl.BlockSpec(memory_space=VMEM)] * 2,
        out_specs=(pl.BlockSpec(memory_space=pltpu.HBM),) * 2,
        scratch_shapes=[pltpu.SemaphoreType.DMA((2,))],
        compiler_params=pltpu.CompilerParams(vmem_limit_bytes=1 << 20),
        name="store",
    )(share, fresh)


def body(rows_n, cols_n, object_field, probe_field, amplitudes, row_offset, col_offset, counts):
    frame = probe_field.shape[0]
    first, second = dft_tables(frame)
    extras = (row_offset, col_offset, amplitudes, first, second)
    obj, probe, acc, *extras = halo(object_field, probe_field, extras, rows_n, cols_n)
    rows, cols, amplitudes, first, second = extras
    acc, back, patch = frames(rows, cols, counts, obj, probe, amplitudes, first, second, acc)
    with_probe = frame % (2 * rows_n * cols_n * 16) == 0
    object_new, fresh = merge(
        acc, back, patch, probe, object_field, rows_n, cols_n, with_probe
    )
    if not with_probe:
        x_re, x_im = back[:, :, :frame], back[:, :, frame:]
        o_re, o_im = patch[:, 0].astype(F32), patch[:, 1].astype(F32)
        grad = [o_re * x_re + o_im * x_im, o_re * x_im - o_im * x_re]
        sums = jnp.stack([x.sum(0) for x in (*grad, o_re * o_re + o_im * o_im)])
        sums = lax.psum(sums, ("row", "col", "mode"))
        fresh = probe + sums[:2] / (sums[2:] + REGULARIZER)
        fresh = jnp.moveaxis(fresh, 0, 1)
    return store(object_new, fresh)


def solution(mesh):
    split = ("groups", "row", "col", "mode")
    placed = (
        P(("groups", "row"), None, "col"),
        P("groups", None, None),
        P(split, None, None),
        P(split),
        P(split),
        P(split),
    )
    return jax.shard_map(
        functools.partial(body, mesh.shape["row"], mesh.shape["col"]),
        mesh=mesh,
        in_specs=placed,
        out_specs=(P(("groups", "row", "mode"), None, "col"), P("groups", None, None)),
        check_vma=False,
    )
```

```python
import functools
import math

import jax
import jax.numpy as jnp
import numpy as np
from jax import lax
from jax.experimental import pallas as pl
from jax.experimental.pallas import tpu as pltpu
from jax.sharding import PartitionSpec as P

FLOOR_SQUARED = 0.25
EPSILON = 1e-05
REGULARIZER = 1.0
F32 = jnp.float32
BF16 = jnp.bfloat16
MESH = pl.DeviceIdType.MESH
VMEM = pltpu.VMEM
LANES = 128
SHIFT = 64
CODE_BITS = 14
CODE_BIAS = 120
PIECE = 32
AHEAD = 3
STEP = 16


def dft_tables(points):
    index = np.arange(points)
    product = (index[:, None] * index[None, :]) % points
    angle = (2.0 * math.pi / points) * product.astype(np.float32)
    norm = np.float32(1.0 / math.sqrt(points))
    cosine = (np.cos(angle.astype(np.float32)) * norm).astype(np.float32)
    sine = (np.sin(angle.astype(np.float32)) * norm).astype(np.float32)
    first = np.block([[cosine, sine], [-sine, cosine]])
    second = np.block([[cosine, -sine], [sine, cosine]])
    return jnp.asarray(first, BF16), jnp.asarray(second, BF16)


def greet(peers):
    barrier = pltpu.get_barrier_semaphore()
    expected = jnp.int32(0)
    for present, where in peers:
        expected = expected + present.astype(jnp.int32)

        @pl.when(present)
        def _(where=where):
            pl.semaphore_signal(barrier, inc=1, device_id=where, device_id_type=MESH)

    return expected


def remote(src, dst, sems, slot, where):
    return pltpu.make_async_remote_copy(
        src_ref=src,
        dst_ref=dst,
        send_sem=sems.at[0, slot],
        recv_sem=sems.at[1, slot],
        device_id=where,
        device_id_type=MESH,
    )


def halo_kernel(rows_n, cols_n, count, *refs):
    field_hbm, probe_hbm = refs[:2]
    extras = refs[2 : 2 + count]
    obj_ref, planes_ref, acc_ref = refs[2 + count : 5 + count]
    landed = refs[5 + count : 5 + 2 * count]
    field_ref, probe_ref, sems, local = refs[5 + 2 * count :]
    r = lax.axis_index("row")
    c = lax.axis_index("col")
    m = lax.axis_index("mode")
    tile_r, _, tile_c = field_ref.shape
    frame = probe_ref.shape[0]
    half, reach = tile_r // 2, frame - SHIFT
    low = reach // 2
    chunks = tile_r // PIECE
    strips = [
        pl.ds(pl.multiple_of(lax.rem(m * (low // PIECE) + k, chunks) * PIECE, PIECE), PIECE)
        for k in range(chunks)
    ]
    pairs = [(field_hbm.at[strip], field_ref.at[strip]) for strip in strips]
    pairs += [(probe_hbm, probe_ref), *zip(extras, landed)]
    fetches = [pltpu.make_async_copy(a, b, local.at[i]) for i, (a, b) in enumerate(pairs)]
    for fetch in fetches[:chunks]:
        fetch.start()
    has_up, has_down = r > 0, r < rows_n - 1
    has_left, has_right = c > 0, c < cols_n - 1
    sib = {"mode": 1 - m}
    up, down = {"row": r - 1}, {"row": r + 1}
    left, right = {"col": c - 1}, {"col": c + 1}
    always = m >= 0
    below_right = {"row": r + 1, "col": c + 1}
    greet([(always, sib), (has_down, down), (has_right, right), (has_down & has_right, below_right)])
    ups, lefts = has_up.astype(jnp.int32), has_left.astype(jnp.int32)
    expected = 1 + ups + lefts + ups * lefts
    mine = pl.ds(pl.multiple_of(m * half, half), half)
    lift = pl.ds(pl.multiple_of(m * low, 32), low)
    below = pl.ds(pl.multiple_of(tile_r + m * low, 32), low)
    first, rest, edge = pl.ds(0, frame), pl.ds(frame, tile_c - frame), pl.ds(tile_c, frame)

    def part(rows, cols, to_rows, to_cols, slot, where):
        return remote(
            obj_ref.at[:, rows, cols], obj_ref.at[:, to_rows, to_cols], sems, slot, where
        )

    pieces = [pl.ds(pl.multiple_of(m * low + k, PIECE), PIECE) for k in range(0, low, PIECE)]
    landing = [
        pl.ds(pl.multiple_of(tile_r + m * low + k, PIECE), PIECE) for k in range(0, low, PIECE)
    ]
    n = len(pieces)
    up_first = [part(a, first, b, first, k, up) for k, (a, b) in enumerate(zip(pieces, landing))]
    corner = [part(b, first, b, edge, n + k, left) for k, b in enumerate(landing[:-1])]
    across = {"row": r - 1, "col": c - 1}
    corner.append(part(pieces[-1], first, landing[-1], edge, 2 * n - 1, across))
    swap_corner = [part(b, edge, b, edge, 2 * n + k, sib) for k, b in enumerate(landing)]
    to_left = part(mine, first, mine, edge, 3 * n, left)
    up_rest = part(lift, rest, below, rest, 3 * n + 1, up)
    swap_edge = part(mine, edge, mine, edge, 3 * n + 2, sib)
    swap_first = part(below, first, below, first, 3 * n + 3, sib)
    swap_rest = part(below, rest, below, rest, 3 * n + 4, sib)

    def convert(k):
        fetches[k].wait()
        for plane in range(2):
            obj_ref[plane, strips[k], :tile_c] = field_ref[strips[k], plane, :].astype(BF16)

    for k in range(n):
        convert(k)
        if k == 0:
            pl.semaphore_wait(pltpu.get_barrier_semaphore(), expected)

        @pl.when(has_up)
        def _(k=k):
            up_first[k].start()

    @pl.when(has_up & has_left)
    def _():
        corner[-1].start()

    for fetch in fetches[chunks:]:
        fetch.start()
    enough = (tile_r - low) // PIECE
    for k in range(n, enough):
        convert(k)

    @pl.when(has_left)
    def _():
        to_left.start()

    for k in range(enough, chunks):
        convert(k)
    fetches[chunks].wait()
    for plane in range(2):
        planes_ref[plane] = probe_ref[:, plane, :]
    acc_ref[...] = jnp.zeros(acc_ref.shape, F32)

    @pl.when(has_up)
    def _():
        for copy in up_first[:AHEAD]:
            copy.wait_send()
        up_rest.start()

    @pl.when(has_down)
    def _():
        for k in range(n):
            up_first[k].wait_recv()
            if k < n - 1:

                @pl.when(has_left)
                def _(k=k):
                    corner[k].start()

        swap_first.start()

    @pl.when(has_right)
    def _():
        to_left.wait_recv()
        swap_edge.start()

    def turn(k):
        @pl.when(has_right & has_down)
        def _():
            corner[k].wait_recv()
            swap_corner[k].start()

    turn(0)

    @pl.when(has_down)
    def _():
        up_rest.wait_recv()
        swap_rest.start()

    for k in range(1, n):
        turn(k)

    @pl.when(has_right)
    def _():
        swap_edge.wait()

    @pl.when(has_down)
    def _():
        swap_first.wait()
        swap_rest.wait()

        @pl.when(has_left)
        def _():
            for copy in corner[:-1]:
                copy.wait_send()

    @pl.when(has_up & has_left)
    def _():
        corner[-1].wait_send()

    @pl.when(has_left)
    def _():
        to_left.wait_send()

    @pl.when(has_up)
    def _():
        for copy in up_first[AHEAD:]:
            copy.wait_send()
        up_rest.wait_send()

    @pl.when(has_right & has_down)
    def _():
        for copy in swap_corner:
            copy.wait()

    for fetch in fetches[chunks + 1 :]:
        fetch.wait()


def halo(field, probe, extras, rows_n, cols_n):
    tile_r, planes, tile_c = field.shape
    frame = probe.shape[0]
    shape = (planes, tile_r + frame, tile_c + frame)
    in_vmem = pl.BlockSpec(memory_space=VMEM)
    return pl.pallas_call(
        functools.partial(halo_kernel, rows_n, cols_n, len(extras)),
        out_shape=(
            jax.ShapeDtypeStruct(shape, BF16),
            jax.ShapeDtypeStruct((planes, frame, frame), F32),
            jax.ShapeDtypeStruct(shape, F32),
            *(jax.ShapeDtypeStruct(x.shape, x.dtype) for x in extras),
        ),
        in_specs=[pl.BlockSpec(memory_space=pltpu.HBM)] * (2 + len(extras)),
        out_specs=(in_vmem,) * (3 + len(extras)),
        scratch_shapes=[
            VMEM(field.shape, F32),
            VMEM(probe.shape, F32),
            pltpu.SemaphoreType.DMA((2, 5 + 3 * ((frame - SHIFT) // 2 // PIECE))),
            pltpu.SemaphoreType.DMA((tile_r // PIECE + 1 + len(extras),)),
        ],
        cost_estimate=pl.CostEstimate(flops=0, bytes_accessed=40 << 20, transcendentals=0),
        compiler_params=pltpu.CompilerParams(
            collective_id=0, has_side_effects=True, vmem_limit_bytes=8 << 20
        ),
        name="halo",
    )(*(pltpu.with_memory_space_constraint(x, pltpu.HBM) for x in (field, probe, *extras)))


def frames_kernel(
    row_ref, col_ref, count_ref, obj, probe_ref, amp_ref, first_ref, second_ref, _zero,
    acc, field, patch, tall, wide,
):
    frame = probe_ref.shape[1]
    ext_rows, ext_cols = obj.shape[1:]
    top = lax.axis_index("row") * (ext_rows - frame)
    left = lax.axis_index("col") * (ext_cols - frame)
    step = 64
    chunks = range(0, frame, step)
    tiles = frame // LANES
    lane = lax.broadcasted_iota(jnp.int32, (step, LANES), 1)

    def place(slot):
        row = row_ref[slot] - top
        col = col_ref[slot] - left
        return row, (col // LANES) * LANES, col % LANES

    def columns(base, tile):
        return pl.ds(pl.multiple_of(base + tile * LANES, LANES), LANES)

    def enter(slot, at):
        row, base, shift = place(slot)
        for k in chunks:
            rows = pl.ds(pl.multiple_of(row + k, step), step)
            here = pl.ds(k, step)
            for plane in range(2):
                turned = []
                for tile in range(tiles + 1):
                    value = obj[plane, rows, columns(base, tile)].astype(F32)
                    turned.append(pltpu.roll(value, shift, 1))
                for tile in range(tiles):
                    value = jnp.where(lane < LANES - shift, turned[tile], turned[tile + 1])
                    patch[at, plane, here, tile * LANES : (tile + 1) * LANES] = value.astype(BF16)
            o_re, o_im = patch[at, 0, here, :].astype(F32), patch[at, 1, here, :].astype(F32)
            p_re, p_im = probe_ref[0, here, :], probe_ref[1, here, :]
            tall[at, here, :] = (p_re * o_re - p_im * o_im).astype(BF16)
            tall[at, frame + k : frame + k + step, :] = (p_re * o_im + p_im * o_re).astype(BF16)

    def transform(at, one_ref, two_ref):
        half = jnp.dot(one_ref[...], tall[at], preferred_element_type=F32).astype(BF16)
        wide[at, :, :frame] = half[:frame]
        wide[at, :, frame:] = half[frame:]
        field[at] = jnp.dot(wide[at], two_ref[...], preferred_element_type=F32)

    def constrain(slot, at):
        for k in chunks:
            here = pl.ds(k, step)
            f_re = field[at, here, :frame]
            f_im = field[at, here, frame:]
            amp = amp_ref[slot, here, :].astype(F32)
            power = f_re * f_re + f_im * f_im
            factor = amp * lax.rsqrt(jnp.maximum(power, FLOOR_SQUARED)) - 1.0
            tall[at, here, :] = (f_re * factor).astype(BF16)
            tall[at, frame + k : frame + k + step, :] = (f_im * factor).astype(BF16)

    def leave(slot, at):
        row, base, shift = place(slot)
        for k in chunks:
            rows = pl.ds(pl.multiple_of(row + k, step), step)
            here = pl.ds(k, step)
            x_re = field[at, here, :frame]
            x_im = field[at, here, frame:]
            p_re, p_im = probe_ref[0, here, :], probe_ref[1, here, :]
            for plane, value in enumerate((p_re * x_re + p_im * x_im, p_re * x_im - p_im * x_re)):
                turned = [
                    pltpu.roll(value[:, t * LANES : (t + 1) * LANES], shift, 1) for t in range(tiles)
                ]
                for tile in range(tiles + 1):
                    if tile == 0:
                        part = jnp.where(lane >= shift, turned[0], 0.0)
                    elif tile == tiles:
                        part = jnp.where(lane < shift, turned[-1], 0.0)
                    else:
                        part = jnp.where(lane < shift, turned[tile - 1], turned[tile])
                    acc[plane, rows, columns(base, tile)] += part

    def run(slots):
        for at, slot in enumerate(slots):
            enter(slot, at)
            transform(at, first_ref, second_ref)
        for at, slot in enumerate(slots):
            constrain(slot, at)
            transform(at, second_ref, first_ref)
        for at, slot in enumerate(slots):
            leave(slot, at)

    def choice(live):
        @pl.when(count_ref[0] == live)
        def _():
            run(range(live))
            for at in range(live, amp_ref.shape[0]):
                field[at] = jnp.zeros(field.shape[1:], F32)
                patch[at] = jnp.zeros(patch.shape[1:], BF16)

    for live in range(1, amp_ref.shape[0] + 1):
        choice(live)


def frames(row_offset, col_offset, counts, obj, probe, amplitudes, first, second, acc):
    frame = probe.shape[1]
    slots = amplitudes.shape[0]
    in_vmem = pl.BlockSpec(memory_space=VMEM)
    in_smem = pl.BlockSpec(memory_space=pltpu.SMEM)
    return pl.pallas_call(
        frames_kernel,
        out_shape=(
            jax.ShapeDtypeStruct(acc.shape, F32),
            jax.ShapeDtypeStruct((slots, frame, 2 * frame), F32),
            jax.ShapeDtypeStruct((slots, 2, frame, frame), BF16),
        ),
        in_specs=[in_smem] * 3 + [in_vmem] * 6,
        out_specs=(in_vmem, in_vmem, in_vmem),
        input_output_aliases={8: 0},
        scratch_shapes=[
            VMEM((slots, 2 * frame, frame), BF16),
            VMEM((slots, frame, 2 * frame), BF16),
        ],
        compiler_params=pltpu.CompilerParams(vmem_limit_bytes=14 << 20),
        name="frames",
    )(row_offset, col_offset, counts, obj, probe, amplitudes, first, second, acc)


def encode(value):
    rows = lax.broadcasted_iota(jnp.int32, value.shape, value.ndim - 2)
    peak = jnp.max(jnp.abs(value), axis=-2, keepdims=True)
    power = jnp.ceil(jnp.log2(jnp.maximum(peak, 1e-30)) + 0.01)
    bits = (power.astype(jnp.int32) + CODE_BIAS) >> (rows % 8)
    whole = jnp.round(value * jnp.exp2(CODE_BITS - power)).astype(jnp.int32)
    return (2 * whole + (bits & 1)).astype(jnp.int16)


def decode(code):
    code = code.astype(jnp.int32)
    rows = lax.broadcasted_iota(jnp.int32, code.shape, code.ndim - 2)
    low = code & 1
    bits = jnp.where(rows < 8, low << (rows % 8), 0)
    power = jnp.sum(bits, axis=-2, keepdims=True) - CODE_BIAS
    return (code - low).astype(F32) * jnp.exp2(power.astype(F32) - (CODE_BITS + 1))


def merge_kernel(
    rows_n, cols_n, with_probe, acc_ref, back_ref, patch_ref, probe_ref, field_ref, share_ref, out_ref,
    sum_ref, got_corner, got_low, got_edge, got_top, total, low_left,
    right_corner, left_corner, right_edge, left_edge, to_down, from_up,
    got_sum, give, gotten, mine_code, sib_code, sems, psems, asems, fsems,
    pair_in, all_in,
):
    r = lax.axis_index("row")
    c = lax.axis_index("col")
    m = lax.axis_index("mode")
    half, _, tile_c = share_ref.shape
    tile_r = 2 * half
    frame = probe_ref.shape[1]
    near = frame - SHIFT - half
    has_up, has_down = r > 0, r < rows_n - 1
    has_left, has_right = c > 0, c < cols_n - 1
    whole = m == 0
    sib = {"mode": 1 - m}
    up, down = {"row": r - 1}, {"row": r + 1}
    left, right = {"col": c - 1}, {"col": c + 1}
    always = m >= 0
    steps = [(a, b) for a in range(rows_n) for b in range(cols_n) if a or b]
    places = [(lax.rem(r + a, rows_n), lax.rem(c + b, cols_n)) for a, b in steps]
    peers = [{"row": a, "col": b} for a, b in places]
    if with_probe:
        others = [(always, p) for p in peers]
    else:
        others = [(has_up, up), (has_down, down), (has_left, left), (has_right, right)]
    barrier = pltpu.get_barrier_semaphore()

    @pl.when(m == 1)
    def _():
        pl.semaphore_signal(barrier, inc=1, device_id=sib, device_id_type=MESH)

    expected = 2 * greet([(present, {**where, "mode": 1}) for present, where in others])

    def block(which, base):
        return pl.ds(pl.multiple_of(which * half + base, half), half)

    top_mine, low_mine = block(m, 0), block(m, tile_r)
    top_sib, low_sib = block(1 - m, 0), block(1 - m, tile_r)
    body, edge = pl.ds(0, tile_c), pl.ds(tile_c, frame)
    first, rest = pl.ds(0, frame), pl.ds(frame, tile_c - frame)
    near_rows, far_rows = pl.ds(0, near), pl.ds(near, half - near)
    sum_rows = frame // 2
    shard = sum_rows // (rows_n * cols_n)

    def chip(row, col):
        return row * cols_n + col

    def rows_of(row, col, base=0):
        return pl.ds(pl.multiple_of(base + chip(row, col) * shard, shard), shard)

    def add_up(base):
        for k in range(0, sum_rows, STEP):
            here = pl.ds(pl.multiple_of(base + k, STEP), STEP)
            grad_re = grad_im = weight = 0.0
            for at in range(patch_ref.shape[0]):
                x_re = back_ref[at, here, :frame]
                x_im = back_ref[at, here, frame:]
                o_re = patch_ref[at, 0, here, :].astype(F32)
                o_im = patch_ref[at, 1, here, :].astype(F32)
                grad_re = grad_re + (o_re * x_re + o_im * x_im)
                grad_im = grad_im + (o_re * x_im - o_im * x_re)
                weight = weight + (o_re * o_re + o_im * o_im)
            sum_ref[0, here, :] = grad_re
            sum_ref[1, here, :] = grad_im
            sum_ref[2, here, :] = weight

    if with_probe:
        add_up((1 - m) * sum_rows)

    @pl.when(m == 0)
    def _():
        pl.semaphore_wait(barrier, 1)
        pl.semaphore_signal(pair_in, inc=1, device_id=sib, device_id_type=MESH)

    @pl.when(m == 1)
    def _():
        pl.semaphore_wait(pair_in, 1)

    if with_probe:
        away = pl.ds(pl.multiple_of((1 - m) * sum_rows, sum_rows), sum_rows)
        swap_sum = remote(sum_ref.at[:, away, :], got_sum, psems, 0, sib)
        swap_sum.start()
    swap_corner = remote(acc_ref.at[:, low_sib, edge], got_corner, sems, 0, sib)
    swap_low = remote(acc_ref.at[:, low_sib, body], got_low, sems, 1, sib)
    swap_edge = remote(acc_ref.at[:, top_sib, edge], got_edge, sems, 2, sib)
    swap_top = remote(acc_ref.at[:, top_sib, body], got_top, sems, 3, sib)

    @pl.when(has_right & has_down)
    def _():
        swap_corner.start()

    def swap_others():
        @pl.when(has_down)
        def _():
            swap_low.start()

        @pl.when(has_right)
        def _():
            swap_edge.start()

        swap_top.start()

    if not with_probe:
        swap_others()

    def part(src, dst, rows, cols, slot, where):
        return remote(src.at[:, rows, cols], dst.at[:, rows, cols], sems, slot, where)

    corner_near = part(right_corner, left_corner, near_rows, first, 4, right)
    corner_far = part(right_corner, left_corner, far_rows, first, 5, right)
    side = remote(right_edge, left_edge, sems, 6, right)
    rest_near = part(to_down, from_up, near_rows, rest, 7, down)
    rest_far = part(to_down, from_up, far_rows, rest, 8, down)
    first_near = part(to_down, from_up, near_rows, first, 9, down)
    first_far = part(to_down, from_up, far_rows, first, 10, down)

    def both(near_copy, far_copy, act):
        act(near_copy)

        @pl.when(whole)
        def _():
            act(far_copy)

    start, recv, sent = (lambda x: x.start()), (lambda x: x.wait_recv()), (lambda x: x.wait_send())

    if with_probe:
        own = chip(r, c)
        base = m * sum_rows
        add_up(base)
        swap_sum.wait_recv()
        swap_others()
        for k, (row, col) in enumerate(places):
            value = sum_ref[:, rows_of(row, col, base), :] + got_sum[:, rows_of(row, col), :]
            give[k] = encode(value)

    @pl.when(m == 1)
    def _():
        pl.semaphore_wait(barrier, expected)
        pl.semaphore_signal(all_in, inc=1, device_id=sib, device_id_type=MESH)

    @pl.when(m == 0)
    def _():
        pl.semaphore_wait(all_in, 1)

    if with_probe:
        scatter = []
        for k in range(len(steps)):
            scatter.append(remote(give.at[k], gotten.at[k], psems, 1 + k, peers[k]))
            scatter[-1].start()

    @pl.when(has_right & has_down)
    def _():
        swap_corner.wait_recv()
        right_corner[...] = (acc_ref[:, low_mine, edge] + got_corner[...]).astype(BF16)
        both(corner_near, corner_far, start)

    @pl.when(has_down)
    def _():
        swap_low.wait_recv()
        to_down[:, :, rest] = (acc_ref[:, low_mine, rest] + got_low[:, :, rest]).astype(BF16)
        low_left[...] = acc_ref[:, low_mine, first] + got_low[:, :, first]

    @pl.when(has_right)
    def _():
        swap_edge.wait_recv()
        right_edge[...] = (acc_ref[:, top_mine, edge] + got_edge[...]).astype(BF16)

    swap_top.wait_recv()
    total[...] = acc_ref[:, top_mine, body] + got_top[...]
    peak = probe_ref[0] * probe_ref[0] + probe_ref[1] * probe_ref[1]
    peak = jnp.max(peak, keepdims=True) + EPSILON
    if with_probe:
        for copy in scatter:
            copy.wait_send()

    @pl.when(has_down)
    def _():
        both(rest_near, rest_far, start)

    @pl.when(has_right)
    def _():
        side.start()

    @pl.when(has_left & has_down)
    def _():
        corner_near.wait_recv()
        low_left[:, near_rows, :] += left_corner[:, near_rows, :].astype(F32)

        @pl.when(whole)
        def _():
            corner_far.wait_recv()
            low_left[:, far_rows, :] += left_corner[:, far_rows, :].astype(F32)

    @pl.when(has_down)
    def _():
        to_down[:, :, first] = low_left[...].astype(BF16)
        both(first_near, first_far, start)

    if with_probe:
        value = sum_ref[:, rows_of(r, c, base), :] + got_sum[:, rows_of(r, c), :]
        for k in range(len(steps)):
            scatter[k].wait_recv()
            value = value + decode(gotten[k])
        weight = value[2:] + REGULARIZER
        mine_code[own] = encode(value[:2] / weight)
        spread, crossings = [], []
        for k in range(len(steps)):
            spread.append(remote(mine_code.at[own], mine_code.at[own], asems, k, peers[k]))
            spread[-1].start()
        crossings.append(remote(mine_code.at[own], sib_code.at[own], fsems, 0, sib))
        crossings[0].start()
    else:
        out_ref[...] = jnp.zeros_like(out_ref)

    @pl.when(has_left)
    def _():
        side.wait_recv()
        total[:, :, first] += left_edge[...].astype(F32)

    @pl.when(has_up)
    def _():
        rest_near.wait_recv()
        first_near.wait_recv()
        total[:, near_rows, :] += from_up[:, near_rows, :].astype(F32)

        @pl.when(whole)
        def _():
            rest_far.wait_recv()
            first_far.wait_recv()
            total[:, far_rows, :] += from_up[:, far_rows, :].astype(F32)

    for plane in range(2):
        share_ref[:, plane, :] = field_ref[top_mine, plane, :] + total[plane] / peak

    if with_probe:

        def finish(codes, row, col, base):
            rows = rows_of(row, col, base)
            fresh = probe_ref[:, rows, :] + decode(codes[chip(row, col)])
            for plane in range(2):
                out_ref[rows, plane, :] = fresh[plane]

        origins = [(lax.rem(r + rows_n - a, rows_n), lax.rem(c + cols_n - b, cols_n)) for a, b in steps]
        for k, (row, col) in enumerate(origins):
            spread[k].wait_recv()
            at = chip(row, col)
            crossings.append(remote(mine_code.at[at], sib_code.at[at], fsems, 1 + k, sib))
            crossings[-1].start()
        for row, col in [(r, c)] + origins:
            finish(mine_code, row, col, base)
        for k, (row, col) in enumerate([(r, c)] + origins):
            crossings[k].wait_recv()
            finish(sib_code, row, col, sum_rows - base)

    swap_top.wait_send()

    @pl.when(has_right)
    def _():
        swap_edge.wait_send()
        side.wait_send()

    @pl.when(has_down)
    def _():
        swap_low.wait_send()
        both(rest_near, rest_far, sent)
        both(first_near, first_far, sent)

    @pl.when(has_right & has_down)
    def _():
        swap_corner.wait_send()
        both(corner_near, corner_far, sent)

    if with_probe:
        swap_sum.wait_send()
        for copy in spread + crossings:
            copy.wait_send()


def merge(acc, back, patch, probe, field, rows_n, cols_n, with_probe):
    tile_r, _, tile_c = field.shape
    frame = probe.shape[1]
    half = tile_r // 2
    sum_rows = frame // 2
    chips = rows_n * cols_n if with_probe else 2
    shard = sum_rows // chips if with_probe else 16
    in_vmem = pl.BlockSpec(memory_space=VMEM)
    return pl.pallas_call(
        functools.partial(merge_kernel, rows_n, cols_n, with_probe),
        out_shape=(
            jax.ShapeDtypeStruct((half, 2, tile_c), F32),
            jax.ShapeDtypeStruct((frame, 2, frame), F32),
        ),
        in_specs=[in_vmem] * 5,
        out_specs=(in_vmem, in_vmem),
        scratch_shapes=[
            VMEM((3, frame, frame), F32),
            VMEM((2, half, frame), F32),
            VMEM((2, half, tile_c), F32),
            VMEM((2, half, frame), F32),
            VMEM((2, half, tile_c), F32),
            VMEM((2, half, tile_c), F32),
            VMEM((2, half, frame), F32),
            VMEM((2, half, frame), BF16),
            VMEM((2, half, frame), BF16),
            VMEM((2, half, frame), BF16),
            VMEM((2, half, frame), BF16),
            VMEM((2, half, tile_c), BF16),
            VMEM((2, half, tile_c), BF16),
            VMEM((3, sum_rows, frame), F32),
            VMEM((chips - 1, 3, shard, frame), jnp.int16),
            VMEM((chips - 1, 3, shard, frame), jnp.int16),
            VMEM((chips, 2, shard, frame), jnp.int16),
            VMEM((chips, 2, shard, frame), jnp.int16),
            pltpu.SemaphoreType.DMA((2, 11)),
            pltpu.SemaphoreType.DMA((2, chips)),
            pltpu.SemaphoreType.DMA((2, chips)),
            pltpu.SemaphoreType.DMA((2, chips)),
            pltpu.SemaphoreType.REGULAR,
            pltpu.SemaphoreType.REGULAR,
        ],
        compiler_params=pltpu.CompilerParams(
            collective_id=1, has_side_effects=True, vmem_limit_bytes=16 << 20
        ),
        name="merge",
    )(acc, back, patch, probe, field)


def store_kernel(share_ref, fresh_ref, share_hbm, fresh_hbm, sems):
    pairs = [(share_ref, share_hbm), (fresh_ref, fresh_hbm)]
    copies = [pltpu.make_async_copy(a, b, sems.at[i]) for i, (a, b) in enumerate(pairs)]
    for copy in copies:
        copy.start()
    for copy in copies:
        copy.wait()


def store(share, fresh):
    return pl.pallas_call(
        store_kernel,
        out_shape=tuple(jax.ShapeDtypeStruct(x.shape, x.dtype) for x in (share, fresh)),
        in_specs=[pl.BlockSpec(memory_space=VMEM)] * 2,
        out_specs=(pl.BlockSpec(memory_space=pltpu.HBM),) * 2,
        scratch_shapes=[pltpu.SemaphoreType.DMA((2,))],
        compiler_params=pltpu.CompilerParams(vmem_limit_bytes=1 << 20),
        name="store",
    )(share, fresh)


def body(rows_n, cols_n, object_field, probe_field, amplitudes, row_offset, col_offset, counts):
    frame = probe_field.shape[0]
    first, second = dft_tables(frame)
    extras = (row_offset, col_offset, amplitudes, first, second)
    obj, probe, acc, *extras = halo(object_field, probe_field, extras, rows_n, cols_n)
    rows, cols, amplitudes, first, second = extras
    acc, back, patch = frames(rows, cols, counts, obj, probe, amplitudes, first, second, acc)
    with_probe = frame % (2 * rows_n * cols_n * 16) == 0
    object_new, fresh = merge(
        acc, back, patch, probe, object_field, rows_n, cols_n, with_probe
    )
    if not with_probe:
        x_re, x_im = back[:, :, :frame], back[:, :, frame:]
        o_re, o_im = patch[:, 0].astype(F32), patch[:, 1].astype(F32)
        grad = [o_re * x_re + o_im * x_im, o_re * x_im - o_im * x_re]
        sums = jnp.stack([x.sum(0) for x in (*grad, o_re * o_re + o_im * o_im)])
        sums = lax.psum(sums, ("row", "col", "mode"))
        fresh = probe + sums[:2] / (sums[2:] + REGULARIZER)
        fresh = jnp.moveaxis(fresh, 0, 1)
    return store(object_new, fresh)


def solution(mesh):
    split = ("groups", "row", "col", "mode")
    placed = (
        P(("groups", "row"), None, "col"),
        P("groups", None, None),
        P(split, None, None),
        P(split),
        P(split),
        P(split),
    )
    return jax.shard_map(
        functools.partial(body, mesh.shape["row"], mesh.shape["col"]),
        mesh=mesh,
        in_specs=placed,
        out_specs=(P(("groups", "row", "mode"), None, "col"), P("groups", None, None)),
        check_vma=False,
    )
```
